32 devices in a mesh: blk: 8 (over z, x), grp: 4 (over y, core).
Axes of the slice: x: 2, y: 2, z: 4, core: 2. Of those that a mesh axis runs over, the one named last changes fastest.
Arguments:
- queries: bfloat16 [16384, 512], P(('blk', 'grp')), may hold values from -64 to 64
- keys: bfloat16 [16384, 128], P(('blk', 'grp')), may hold values from -8 to 8
- values: bfloat16 [16384, 128], P(('blk', 'grp')), may hold values from -6 to 6
- selected: int32 [32, 16], replicated, may hold values from 0 to 255, as said below
- key_in: bfloat16 [4096, 256], replicated, may hold values from -0.09375 to 0.09375
- key_out: bfloat16 [256, 128], replicated, may hold values from -0.375 to 0.375
- value_in: bfloat16 [4096, 256], replicated, may hold values from -0.09375 to 0.09375
- value_out: bfloat16 [256, 128], replicated, may hold values from -0.375 to 0.375
- positions: bfloat16 [2, 32, 128], replicated, may hold values from -5 to 5
- gate_weight: bfloat16 [512, 12], replicated, may hold values from -0.25 to 0.25
Outputs:
- attended: bfloat16 [16384, 512], P(('blk', 'grp'))
The draws below stay inside these ranges and needn't reach their ends.
Inputs may be any that keep to these rules, and one draw needn't show every extreme that they name: `selected`: row d lists 16 different fine blocks. Write r = 32 and b = d // 4. Entry 0 is the first fine block of group d's own tokens. Every listed block j with j // r different from b has j // r < b, and no two listed blocks share a value of j // r other than b. Blocks with j // r == b may lie after group d's tokens.
All inputs are finite; a program needn't handle non-finite values.
Results may differ from the reference program's by a relative error of at most 0.004.
Values may be sent and summed in bfloat16 or wider, within the bound.
A program may use at most 64 MiB of HBM per device.

```python
import jax
import jax.numpy as jnp
from jax import lax

HEAD_DIM = 128
HEADS = 4
CMP_HIDDEN = 256
CMP_BLOCK = 32
SEL_BLOCK = 64
TOPN = 16
WINDOW = 512
TOK_DEV = 512
SEQ = 16384
NCMP = 512
GROUPS = 32
N_BLK = 8
N_GRP = 4


def keys_law(key):
    base_key = jax.random.fold_in(key, 11)
    second_key = jax.random.fold_in(base_key, 1)
    return jnp.clip(jax.random.normal(second_key, (SEQ, HEAD_DIM), jnp.float32), -6.0, 6.0)


def draw_keys(key, part):
    return keys_law(key).astype(jnp.bfloat16)


def draw_queries(key, part):
    own_key = jax.random.fold_in(key, 5)
    base = jnp.clip(jax.random.normal(own_key, (SEQ, HEADS * HEAD_DIM), jnp.float32), -6.0, 6.0)
    return base.astype(jnp.bfloat16)


def draw_selected(key, part):
    groups = N_BLK * N_GRP
    per_row = N_GRP * TOK_DEV // SEL_BLOCK
    base_key = jax.random.fold_in(key, 23)
    key_rows, key_blocks, key_own = jax.random.split(base_key, 3)
    group_ids = jnp.arange(groups, dtype=jnp.int32)
    group_row = group_ids // N_GRP
    group_col = group_ids % N_GRP
    row_ids = jnp.arange(N_BLK, dtype=jnp.int32)
    row_score = jax.random.randint(key_rows, (groups, N_BLK), 1, 1 << 20) * N_BLK + row_ids[None, :]
    row_score = jnp.where(row_ids[None, :] == 0, 1 << 28, row_score)
    eligible = row_ids[None, :] < group_row[:, None]
    row_score = jnp.where(eligible, row_score, -1)
    rank = jnp.sum((row_score[:, None, :] > row_score[:, :, None]).astype(jnp.int32), axis=2)
    chosen = eligible & (rank < TOPN - 1)
    remote_count = jnp.sum(chosen.astype(jnp.int32), axis=1)
    slots = jnp.arange(TOPN - 1, dtype=jnp.int32)
    hit = chosen[:, None, :] & (rank[:, None, :] == slots[None, :, None])
    row_of_slot = jnp.sum(jnp.where(hit, row_ids[None, None, :], 0), axis=2)
    remote_blocks = row_of_slot * per_row + jax.random.randint(key_blocks, (groups, TOPN - 1), 0, per_row)
    first_local = group_col * (TOK_DEV // SEL_BLOCK)
    local_ids = jnp.arange(per_row, dtype=jnp.int32)
    own_score = jax.random.randint(key_own, (groups, per_row), 0, 1 << 20) * per_row + local_ids[None, :]
    own_score = jnp.where(local_ids[None, :] == first_local[:, None], -1, own_score)
    best_scores, unused = jax.lax.top_k(own_score, TOPN - 1)
    own_extra = group_row[:, None] * per_row + best_scores % per_row
    own_index = jnp.clip(slots[None, :] - remote_count[:, None], 0, TOPN - 2)
    own_pick = jnp.take_along_axis(own_extra, own_index, axis=1)
    tail = jnp.where(slots[None, :] < remote_count[:, None], remote_blocks, own_pick)
    head = (group_row * per_row + first_local)[:, None]
    return jnp.concatenate([head, tail], axis=1).astype(jnp.int32)


def level_of(key, extent, cuts, low, high):
    def one(axis_at, shards_of):
        heights = jax.random.uniform(jax.random.fold_in(jax.random.fold_in(key, 6), axis_at), (shards_of,), jnp.float32, low / len(cuts), high / len(cuts))
        return jnp.repeat(jnp.exp(heights), extent[axis_at] // shards_of).reshape((-1,) + (1,) * (len(extent) - axis_at - 1))

    level = one(*cuts[0])
    for cut in cuts[1:]:
        level = level * one(*cut)
    return level


def centred(rng, shape, deviation, limit, cuts=(), kind=jnp.bfloat16):
    values = jax.random.normal(rng, shape, jnp.float32) * deviation
    if len(cuts) > 0:
        values = level_of(rng, shape, cuts, -0.22, 0.18) * values
    return jnp.clip(values, min=-limit, max=limit).astype(kind)


def setup_inputs(seed: int = 0) -> dict:
    streams_of = jax.random.split(jax.random.key(seed), 11)
    queries = draw_queries(jax.random.fold_in(streams_of[10], 71), 0)
    keys = draw_keys(jax.random.fold_in(streams_of[10], 71), 0)
    values = centred(streams_of[2], (SEQ, HEAD_DIM), 1.0, 6.0, ((0, 32),))
    selected = draw_selected(jax.random.fold_in(streams_of[10], 71), 0)
    key_in = centred(streams_of[4], (CMP_BLOCK * HEAD_DIM, CMP_HIDDEN), (CMP_BLOCK * HEAD_DIM) ** -0.5, 0.09375)
    key_out = centred(streams_of[5], (CMP_HIDDEN, HEAD_DIM), CMP_HIDDEN ** -0.5, 0.375)
    value_in = centred(streams_of[6], (CMP_BLOCK * HEAD_DIM, CMP_HIDDEN), (CMP_BLOCK * HEAD_DIM) ** -0.5, 0.09375)
    value_out = centred(streams_of[7], (CMP_HIDDEN, HEAD_DIM), CMP_HIDDEN ** -0.5, 0.375)
    positions = centred(streams_of[8], (2, CMP_BLOCK, HEAD_DIM), 1.0, 5.0)
    gate_weight = centred(streams_of[9], (HEADS * HEAD_DIM, 3 * HEADS), (HEADS * HEAD_DIM) ** -0.5, 0.25)
    return dict(queries=queries, keys=keys, values=values, selected=selected, key_in=key_in, key_out=key_out, value_in=value_in, value_out=value_out, positions=positions, gate_weight=gate_weight)


NEG = -1e30


def compress(tokens, shift, w_in, w_out):
    count = tokens.shape[0] // CMP_BLOCK
    mixed = tokens.astype(jnp.float32).reshape(count, CMP_BLOCK, HEAD_DIM) + shift.astype(jnp.float32)[None]
    flat = mixed.astype(jnp.bfloat16).reshape(count, CMP_BLOCK * HEAD_DIM)
    hidden = jax.nn.silu(jnp.dot(flat, w_in, preferred_element_type=jnp.float32)).astype(jnp.bfloat16)
    return jnp.dot(hidden, w_out, preferred_element_type=jnp.float32).astype(jnp.bfloat16)


def attend(query_rows, query_pos, key_rows, value_rows, key_pos, span):
    scale = HEAD_DIM ** -0.5
    scores = jnp.einsum("qhd,kd->qhk", query_rows.astype(jnp.float32), key_rows.astype(jnp.float32)) * scale
    allowed = (key_pos[None, :] <= query_pos[:, None]) & (key_pos[None, :] > query_pos[:, None] - span) & (key_pos[None, :] >= 0)
    scores = jnp.where(allowed[:, None, :], scores, NEG)
    top = jnp.max(scores, axis=2, keepdims=True)
    weights = jnp.exp(scores - top)
    total = jnp.sum(weights, axis=2)
    mixed = jnp.einsum("qhk,kd->qhd", weights.astype(jnp.bfloat16).astype(jnp.float32), value_rows.astype(jnp.float32))
    return mixed / total[..., None]


def reference(queries, keys, values, selected, key_in, key_out, value_in, value_out, positions, gate_weight):
    scale = HEAD_DIM ** -0.5
    comp_keys = compress(keys, positions[0], key_in, key_out)
    comp_values = compress(values, positions[1], value_in, value_out)
    comp_end = jnp.arange(NCMP, dtype=jnp.int32) * CMP_BLOCK + (CMP_BLOCK - 1)
    padded_keys = jnp.concatenate([jnp.zeros((WINDOW, HEAD_DIM), keys.dtype), keys], axis=0)
    padded_values = jnp.concatenate([jnp.zeros((WINDOW, HEAD_DIM), values.dtype), values], axis=0)

    def group(index):
        first = index * TOK_DEV
        flat_rows = lax.dynamic_slice_in_dim(queries, first, TOK_DEV, 0)
        rows = flat_rows.reshape(TOK_DEV, HEADS, HEAD_DIM)
        query_pos = first + jnp.arange(TOK_DEV, dtype=jnp.int32)
        scores = jnp.einsum("qhd,kd->qhk", rows.astype(jnp.float32), comp_keys.astype(jnp.float32)) * scale
        seen = comp_end[None, :] <= query_pos[:, None]
        scores = jnp.where(seen[:, None, :], scores, NEG)
        top = jnp.maximum(jnp.max(scores, axis=2, keepdims=True), 0.0)
        weights = jnp.exp(scores - top)
        total = jnp.exp(-top[..., 0]) + jnp.sum(weights, axis=2)
        coarse = jnp.einsum("qhk,kd->qhd", weights.astype(jnp.bfloat16).astype(jnp.float32), comp_values.astype(jnp.float32)) / total[..., None]
        chosen = lax.dynamic_index_in_dim(selected, index, 0, keepdims=False)
        token_ids = (chosen[:, None] * SEL_BLOCK + jnp.arange(SEL_BLOCK, dtype=jnp.int32)[None, :]).reshape(-1)
        fine = attend(rows, query_pos, jnp.take(keys, token_ids, axis=0), jnp.take(values, token_ids, axis=0), token_ids, SEQ + 1)
        window_keys = lax.dynamic_slice_in_dim(padded_keys, first, TOK_DEV + WINDOW, 0)
        window_values = lax.dynamic_slice_in_dim(padded_values, first, TOK_DEV + WINDOW, 0)
        window_pos = first - WINDOW + jnp.arange(TOK_DEV + WINDOW, dtype=jnp.int32)
        local = attend(rows, query_pos, window_keys, window_values, window_pos, WINDOW)
        gates = jax.nn.sigmoid(jnp.dot(flat_rows, gate_weight, preferred_element_type=jnp.float32)).reshape(TOK_DEV, 3, HEADS)
        mixed = gates[:, 0, :, None] * coarse + gates[:, 1, :, None] * fine + gates[:, 2, :, None] * local
        return mixed.astype(jnp.bfloat16).reshape(TOK_DEV, HEADS * HEAD_DIM)

    result = lax.map(group, jnp.arange(GROUPS, dtype=jnp.int32))
    return result.reshape(SEQ, HEADS * HEAD_DIM)
```

```python
import functools
import math

import jax
import jax.numpy as jnp
from jax import lax
from jax.experimental import pallas as pl
from jax.experimental.pallas import tpu as pltpu
from jax.sharding import PartitionSpec as P

HEAD_DIM = 128
HEADS = 4
CMP_BLOCK = 32
SEL_BLOCK = 64
TOPN = 16
WINDOW = 512
ROWS = 128
LANES = HEADS * ROWS

FAR = 1e30
RATE = HEAD_DIM**-0.5 * math.log2(math.e)
MESH = pl.DeviceIdType.MESH
F32 = jnp.float32
BF16 = jnp.bfloat16


def across(a, b):
    return lax.dot_general(a, b, (((1,), (1,)), ((), ())), preferred_element_type=F32)


def scores(k, q):
    return across(jnp.concatenate([k, k], axis=1), q)


def rows8(s):
    return s.reshape(s.shape[0] // 8, 8, s.shape[1])


def peak(parts, hides):
    tops = []
    for s, hide in zip(parts, hides):
        top = jnp.max(rows8(s), axis=0)
        tops.append(top if hide is None else top - hide)
    return jnp.max(functools.reduce(jnp.maximum, tops), axis=0, keepdims=True)


def weigh(parts, hides, top):
    packed, sums = [], []
    for s, hide in zip(parts, hides):
        w = jnp.exp2(s - (top if hide is None else top + hide))
        packed.append(w.astype(BF16))
        sums.append(jnp.sum(rows8(w), axis=0))
    total = jnp.sum(functools.reduce(jnp.add, sums), axis=0, keepdims=True)
    return jnp.concatenate(packed, axis=0), total


def times(vt, w):
    return jnp.dot(vt, w, preferred_element_type=F32)


def merge_sort(keys):
    keys = list(keys)
    n = len(keys)
    p = 1
    while p < n:
        k = p
        while k >= 1:
            for j in range(k % p, n - k, 2 * k):
                for i in range(min(k, n - j - k)):
                    if (i + j) // (p * 2) == (i + j + k) // (p * 2):
                        lo, hi = keys[i + j], keys[i + j + k]
                        keys[i + j] = jnp.minimum(lo, hi)
                        keys[i + j + k] = jnp.maximum(lo, hi)
            k //= 2
        p *= 2
    return keys


def kernel(
    B,
    G,
    sel_in,
    queries_in,
    keys_in,
    values_in,
    key_in,
    key_out,
    value_in,
    value_out,
    positions_in,
    gate_weight_in,
    out,
    sel,
    queries,
    positions,
    gate_weight,
    w_in,
    w_out,
    shifted,
    sk,
    sv,
    pk,
    pv,
    ik,
    iv,
    stk,
    stv,
    cc,
    cvt,
    qs,
    wvt,
    pvt,
    fk,
    fvt,
    bias,
    acc,
    part,
    stat,
    gates,
    l_sem,
    w_sem,
    a_s,
    a_r,
    m_s,
    m_r,
    p_s,
    p_r,
    b_s,
    b_r,
    c_s,
    c_r,
    f_s,
    f_r,
    ready,
    ready_head,
):
    T = queries.shape[0]
    N = T // CMP_BLOCK
    Y = G // 2
    STEPS = T // ROWS
    own_blocks = T // SEL_BLOCK
    per_row = G * own_blocks
    near_count = min(max(TOPN - (B - 1), 0), own_blocks)
    b = lax.axis_index("blk")
    g = lax.axis_index("grp")
    y = g // 2
    core = g % 2
    mate = g + 1 - 2 * core
    position = b * G + g
    first = position * T

    row = (sk, sv)
    prev = (pk, pv)
    staged = (stk, stv)
    inbox = (ik, iv)

    def slot(column):
        return pl.ds(column * own_blocks, own_blocks)

    def local(src, dst, sem):
        return pltpu.make_async_copy(src, dst, sem)

    def remote(src, dst, send, recv, dev):
        return pltpu.make_async_remote_copy(
            src_ref=src,
            dst_ref=dst,
            send_sem=send,
            recv_sem=recv,
            device_id=dev,
            device_id_type=MESH,
        )

    def at(stretch, column):
        return {"blk": stretch, "grp": column}

    def when(condition):
        return lambda body: pl.when(condition)(body)

    own_load = [
        local(keys_in, sk.at[slot(g)], l_sem.at[0]),
        local(values_in, sv.at[slot(g)], l_sem.at[1]),
    ]
    q_load = local(queries_in, queries, l_sem.at[2])
    gate_load = local(gate_weight_in, gate_weight, l_sem.at[3])
    shift_load = local(positions_in, positions, l_sem.at[4])
    sel_load = local(sel_in, sel, l_sem.at[5])
    weight_loads = [
        local(src, dst, w_sem.at[n])
        for n, (src, dst) in enumerate(
            (
                (key_in, w_in.at[0]),
                (value_in, w_in.at[1]),
                (key_out, w_out.at[0]),
                (value_out, w_out.at[1]),
            )
        )
    ]
    for load in own_load + [q_load, gate_load, shift_load, sel_load] + weight_loads:
        load.start()

    cc[...] = jnp.zeros_like(cc)
    pk[...] = jnp.zeros_like(pk)
    pv[...] = jnp.zeros_like(pv)

    source = jnp.logical_and(g == 1, b < B - 1)
    head = jnp.logical_and(g == 0, b > 0)
    barrier = pltpu.get_barrier_semaphore()

    def greet(dev):
        pl.semaphore_signal(barrier, inc=1, device_id=dev, device_id_type=MESH)

    for e in range(1, G):
        greet(at(b, (g + e) % G))
    for d in range(1, B):

        @when(b + d < B)
        def _(d=d):
            greet(at(b + d, g))

    @when(source)
    def _():
        greet(at(b + 1, 0))

    pl.semaphore_wait(barrier, G - 1 + b + jnp.where(head, 1, 0))

    def over_y(c, e):
        mine = row[c].at[slot(g)]
        return remote(mine, mine, a_s.at[c, e], a_r.at[c, e], at(b, ((y + e) % Y) * 2 + core))

    def to_mate(c, e):
        piece = row[c].at[slot(((y - e + Y) % Y) * 2 + core)]
        return remote(piece, piece, m_s.at[c, e], m_r.at[c, e], at(b, mate))

    def to_next(c):
        return remote(
            row[c].at[slot(G - 1)], prev[c], p_s.at[c], p_r.at[c], at((b + 1) % B, 0)
        )

    def block_out(c, d):
        return remote(
            staged[c].at[d - 1], inbox[c].at[b], b_s.at[c, d], b_r.at[c, d], at((b + d) % B, g)
        )

    mine_rows = pl.ds(pl.multiple_of(b * N, N), N)

    def coarse_out(d):
        piece = cc.at[g, :, mine_rows, :]
        return remote(piece, piece, c_s.at[d], c_r.at[d], at((b + d) % B, g))

    def coarse_over_y(e):
        return remote(
            cc.at[g], cc.at[g], f_s.at[0, e], f_r.at[0, e], at(b, ((y + e) % Y) * 2 + core)
        )

    def coarse_to_mate(e):
        piece = cc.at[((y - e + Y) % Y) * 2 + core]
        return remote(piece, piece, f_s.at[1, e], f_r.at[1, e], at(b, mate))

    for c in range(2):
        own_load[c].wait()
        for e in range(1, Y):
            over_y(c, e).start()
        to_mate(c, 0).start()

    for d in range(1, B):

        @when(b - d >= 0)
        def _(d=d):
            pl.semaphore_signal(ready.at[d], inc=1, device_id=at(b - d, g), device_id_type=MESH)

    @when(head)
    def _():
        pl.semaphore_signal(ready_head, inc=1, device_id=at(b - 1, 1), device_id_type=MESH)

    q_load.wait()
    for step in range(STEPS):
        for h in range(HEADS):
            piece = queries[step * ROWS : (step + 1) * ROWS, h * HEAD_DIM : (h + 1) * HEAD_DIM]
            piece = piece.astype(F32) * RATE
            high = piece.astype(BF16)
            qs[step, h * ROWS : (h + 1) * ROWS, :HEAD_DIM] = high
            qs[step, h * ROWS : (h + 1) * ROWS, HEAD_DIM:] = (piece - high.astype(F32)).astype(BF16)
    gate_load.wait()
    gates[...] = jax.nn.sigmoid(across(gate_weight[...], queries[...]))

    shift_load.wait()
    flat = (T, HEAD_DIM)
    for c in range(2):
        shift = positions[c].astype(F32)
        tokens = row[c][slot(g)].reshape(flat).astype(F32).reshape(N, CMP_BLOCK, HEAD_DIM)
        shifted[c] = (tokens + shift[None]).reshape(flat)
    wvt[...] = sv[slot(g)].reshape(flat).T
    for load in weight_loads:
        load.wait()
    for c in range(2):
        wide = jnp.concatenate(
            [shifted[c, pl.ds(t, N, stride=CMP_BLOCK), :].astype(BF16) for t in range(CMP_BLOCK)],
            axis=1,
        )
        hidden = jax.nn.silu(jnp.dot(wide, w_in[c], preferred_element_type=F32)).astype(BF16)
        cc[g, c, mine_rows, :] = jnp.dot(hidden, w_out[c], preferred_element_type=F32).astype(BF16)

    sel_load.wait()

    def owner_of(j):
        return lax.div(j, per_row)

    def same(left, right):
        gap = left - right
        return 1 - jnp.minimum(jnp.maximum(gap, -gap), 1)

    picks = []
    for d in range(1, B):
        line = jnp.minimum(b + d, B - 1) * G + g
        pick = jnp.int32(0)
        for i in range(TOPN):
            j = sel[i, line]
            pick = pick + same(owner_of(j), b) * (j - b * per_row)
        picks.append(pick)

    order = []
    for i in range(TOPN):
        j = sel[i, position]
        rel = j - b * per_row - g * own_blocks
        wrapped = jnp.where(rel < 0, rel + per_row, rel)
        order.append(jnp.where(j >= b * per_row, wrapped, j + per_row))
    order = merge_sort(order)

    def entry(i):
        code = order[i]
        near = code < per_row
        turned = code + g * own_blocks
        rank = jnp.where(turned >= per_row, turned - per_row, turned)
        rank = jnp.where(near, rank, 0)
        start = jnp.where(near, (b * per_row + rank) * SEL_BLOCK, 0)
        owner = jnp.where(near, 0, owner_of(code - per_row))
        return near, rank, owner, start

    def iotas(count):
        k = lax.broadcasted_iota(jnp.int32, (count, LANES), 0)
        q = lax.broadcasted_iota(jnp.int32, (count, LANES), 1) % ROWS
        return k, q

    def gate(n, step):
        cols = pl.ds(step * ROWS, ROWS)
        return jnp.concatenate(
            [gates[n * HEADS + h : n * HEADS + h + 1, cols] for h in range(HEADS)], axis=1
        )

    def keep(which, step, mixed, top, total):
        part[which, step] = mixed
        stat[which, step, 0:1] = top
        stat[which, step, 1:2] = total

    def join(which, step, mixed, top, total, best):
        old = jnp.exp2(stat[which, step, 0:1] - best)
        return part[which, step] * old + mixed, stat[which, step, 1:2] * old + total

    kd, qd = iotas(ROWS)
    own_keys = sk[slot(g)].reshape(flat)
    for step in range(STEPS):
        count = (step + 1) * ROWS
        s = scores(own_keys[:count], qs[step])
        parts = [jnp.where(kd <= qd, s[count - ROWS :], -FAR)]
        if step > 0:
            parts = [s[: count - ROWS]] + parts
        hides = [None] * len(parts)
        top = peak(parts, hides)
        w, total = weigh(parts, hides, top)
        keep(0, step, times(wvt[:, :count], w), top, total)

    for d in range(B - 1, 0, -1):

        @when(b + d < B)
        def _(d=d):
            pl.semaphore_wait(ready.at[d], 1)
            coarse_out(d).start()

    @when(source)
    def _():
        pl.semaphore_wait(ready_head, 1)

    def relay(c):
        for e in range(1, Y):
            over_y(c, e).wait_recv()
            to_mate(c, e).start()

        @when(source)
        def _():
            to_next(c).start()

    def spread(c):
        for e in range(Y):
            to_mate(c, e).wait_recv()
        for d in range(B - 1, 0, -1):

            @when(b + d < B)
            def _(d=d):
                staged[c][d - 1] = row[c][picks[d - 1]]

        for d in range(B - 1, 0, -1):

            @when(b + d < B)
            def _(d=d):
                block_out(c, d).start()

    relay(0)

    for d in range(1, B):

        @when(b - d >= 0)
        def _(d=d):
            coarse_out(d).wait_recv()

    for e in range(1, Y):
        coarse_over_y(e).start()
    coarse_to_mate(0).start()

    spread(0)

    entries = [entry(i) for i in range(TOPN)]
    for i in range(near_count):
        fk[pl.ds(i * SEL_BLOCK, SEL_BLOCK), :] = sk[entries[i][1]]

    for e in range(1, Y):
        coarse_over_y(e).wait_recv()
        coarse_to_mate(e).start()

    relay(1)

    for e in range(Y):
        coarse_to_mate(e).wait_recv()

    for column in range(G):
        cvt[:, pl.ds(column * B * N, B * N)] = cc[column, 1].T
    cvt[:, pl.ds(G * B * N, ROWS)] = jnp.concatenate(
        [cc[g, 1, mine_rows, :], jnp.zeros((ROWS - N, HEAD_DIM), BF16)], axis=0
    ).T
    k = lax.broadcasted_iota(jnp.int32, (B * N, ROWS), 0)
    for column in range(G):
        seen = (k // N) * G + column < position
        bias[pl.ds(column * B * N, B * N), :] = jnp.where(seen, 0.0, -FAR)
    kc, qc = iotas(N)
    ends = kc * CMP_BLOCK + (CMP_BLOCK - 1) - qc

    def coarse_step(step, carry):
        parts = []
        for column in range(G):
            s = scores(cc[column, 0], qs[step])
            off = bias[pl.ds(column * B * N, B * N), :]
            parts.append(s + jnp.concatenate([off] * HEADS, axis=1))
        s = scores(cc[g, 0, mine_rows, :], qs[step])
        parts.append(jnp.where(ends <= step * ROWS, s, -FAR))
        hides = [None] * len(parts)
        top = jnp.maximum(peak(parts, hides), 0.0)
        w, total = weigh(parts, hides, top)
        w = jnp.concatenate([w, jnp.zeros((ROWS - N, LANES), BF16)], axis=0)
        total = total + jnp.exp2(-top)
        acc[step] = times(cvt[...], w) * (gate(0, step) / total)
        return carry

    half = STEPS // 2
    lax.fori_loop(0, half, coarse_step, 0, unroll=True)
    spread(1)
    lax.fori_loop(half, STEPS, coarse_step, 0, unroll=True)

    ks, qf = iotas(SEL_BLOCK)
    ahead = ks - qf

    def fine_parts(step, low, high):
        s = scores(fk[pl.ds(low * SEL_BLOCK, (high - low) * SEL_BLOCK), :], qs[step])
        parts, hides = [], []
        for i in range(low, high):
            piece = s[(i - low) * SEL_BLOCK : (i - low + 1) * SEL_BLOCK]
            start = entries[i][3]
            if i < own_blocks:
                parts.append(jnp.where(ahead <= first + step * ROWS - start, piece, -FAR))
                hides.append(None)
            else:
                parts.append(piece)
                hides.append(jnp.where(start <= first, 0.0, FAR).astype(F32))
        return parts, hides

    if near_count > 0:
        for i in range(near_count):
            fvt[:, pl.ds(i * SEL_BLOCK, SEL_BLOCK)] = sv[entries[i][1]].T

        def near_step(step, carry):
            parts, hides = fine_parts(step, 0, near_count)
            top = peak(parts, hides)
            w, total = weigh(parts, hides, top)
            keep(1, step, times(fvt[:, : near_count * SEL_BLOCK], w), top, total)
            return carry

        lax.fori_loop(0, STEPS, near_step, 0, unroll=True)

    @when(head)
    def _():
        for c in range(2):
            to_next(c).wait_recv()

    before = slot(jnp.maximum(g - 1, 0))
    prev_keys = jnp.where(g == 0, pk[...], sk[before]).reshape(flat)
    pvt[...] = jnp.where(g == 0, pv[...], sv[before]).reshape(flat).T
    opening = jnp.where(position == 0, FAR, 0.0).astype(F32)
    for step in range(STEPS):
        low = step * ROWS
        s = scores(prev_keys[low:], qs[step])
        parts = [jnp.where(kd > qd, s[:ROWS], -FAR)]
        if step < STEPS - 1:
            parts.append(s[ROWS:])
        hides = [opening] * len(parts)
        top = jnp.maximum(peak(parts, hides), stat[0, step, 0:1])
        w, total = weigh(parts, hides, top)
        mixed, total = join(0, step, times(pvt[:, low:], w), top, total, top)
        acc[step] = acc[step] + mixed * (gate(2, step) / total)

    for c in range(2):
        for d in range(1, B):

            @when(b - d >= 0)
            def _(c=c, d=d):
                block_out(c, d).wait_recv()

    for i in range(near_count, TOPN):
        near, rank, owner, _ = entries[i]
        fk[pl.ds(i * SEL_BLOCK, SEL_BLOCK), :] = jnp.where(near, sk[rank], ik[owner])
        fvt[:, pl.ds(i * SEL_BLOCK, SEL_BLOCK)] = jnp.where(near, sv[rank], iv[owner]).T

    def far_step(step, carry):
        parts, hides = fine_parts(step, near_count, TOPN)
        top = peak(parts, hides)
        if near_count > 0:
            top = jnp.maximum(top, stat[1, step, 0:1])
        w, total = weigh(parts, hides, top)
        mixed = times(fvt[:, near_count * SEL_BLOCK :], w)
        if near_count > 0:
            mixed, total = join(1, step, mixed, top, total, top)
        mixed = acc[step] + mixed * (gate(1, step) / total)
        for h in range(HEADS):
            out[pl.ds(step * ROWS, ROWS), h * HEAD_DIM : (h + 1) * HEAD_DIM] = mixed[
                :, h * ROWS : (h + 1) * ROWS
            ].T.astype(BF16)
        return carry

    lax.fori_loop(0, STEPS, far_step, 0, unroll=True)

    for c in range(2):
        for e in range(1, Y):
            over_y(c, e).wait_send()
        for e in range(Y):
            to_mate(c, e).wait_send()

        @when(source)
        def _(c=c):
            to_next(c).wait_send()

        for d in range(1, B):

            @when(b + d < B)
            def _(c=c, d=d):
                block_out(c, d).wait_send()

    for d in range(1, B):

        @when(b + d < B)
        def _(d=d):
            coarse_out(d).wait_send()

    for e in range(1, Y):
        coarse_over_y(e).wait_send()
    for e in range(Y):
        coarse_to_mate(e).wait_send()


def per_device(
    queries, keys, values, selected, key_in, key_out, value_in, value_out, positions, gate_weight
):
    B = lax.axis_size("blk")
    G = lax.axis_size("grp")
    T = keys.shape[0]
    N = T // CMP_BLOCK
    Y = G // 2
    STEPS = T // ROWS
    own_blocks = T // SEL_BLOCK
    inner, hidden = key_in.shape
    anywhere = pl.BlockSpec(memory_space=pl.ANY)
    dma = pltpu.SemaphoreType.DMA
    regular = pltpu.SemaphoreType.REGULAR

    def buf(*shape, dtype=BF16):
        return pltpu.VMEM(shape, dtype)

    def blocks(count):
        return buf(count, SEL_BLOCK, HEAD_DIM)

    return pl.pallas_call(
        functools.partial(kernel, B, G),
        out_shape=pltpu.VMEM(queries.shape, BF16),
        in_specs=[anywhere] * 10,
        out_specs=pl.BlockSpec(memory_space=pltpu.VMEM),
        scratch_shapes=[
            pltpu.SMEM((TOPN, B * G), jnp.int32),
            buf(*queries.shape),
            buf(*positions.shape),
            buf(gate_weight.shape[1], gate_weight.shape[0]),
            buf(2, inner, hidden),
            buf(2, hidden, HEAD_DIM),
            buf(2, T, HEAD_DIM, dtype=F32),
            blocks(G * own_blocks),
            blocks(G * own_blocks),
            blocks(own_blocks),
            blocks(own_blocks),
            blocks(B),
            blocks(B),
            blocks(B - 1),
            blocks(B - 1),
            buf(G, 2, B * N, HEAD_DIM),
            buf(HEAD_DIM, G * B * N + ROWS),
            buf(STEPS, LANES, 2 * HEAD_DIM),
            buf(HEAD_DIM, T),
            buf(HEAD_DIM, T),
            buf(TOPN * SEL_BLOCK, HEAD_DIM),
            buf(HEAD_DIM, TOPN * SEL_BLOCK),
            buf(G * B * N, ROWS, dtype=F32),
            buf(STEPS, HEAD_DIM, LANES, dtype=F32),
            buf(2, STEPS, HEAD_DIM, LANES, dtype=F32),
            buf(2, STEPS, 8, LANES, dtype=F32),
            buf(3 * HEADS, T, dtype=F32),
            dma((6,)),
            dma((4,)),
            dma((2, Y)),
            dma((2, Y)),
            dma((2, Y)),
            dma((2, Y)),
            dma((2,)),
            dma((2,)),
            dma((2, B)),
            dma((2, B)),
            dma((B,)),
            dma((B,)),
            dma((2, Y)),
            dma((2, Y)),
            regular((B,)),
            regular,
        ],
        compiler_params=pltpu.CompilerParams(
            collective_id=0, has_side_effects=True, vmem_limit_bytes=56 << 20
        ),
    )(
        selected.T,
        queries,
        keys.reshape(T // SEL_BLOCK, SEL_BLOCK, HEAD_DIM),
        values.reshape(T // SEL_BLOCK, SEL_BLOCK, HEAD_DIM),
        key_in,
        key_out,
        value_in,
        value_out,
        positions,
        gate_weight.T,
    )


def solution(mesh):
    rows = P(("blk", "grp"), None)
    return jax.shard_map(
        per_device,
        mesh=mesh,
        in_specs=(rows, rows, rows, P(), P(), P(), P(), P(), P(), P()),
        out_specs=rows,
        check_vma=False,
    )
```

```python
import functools
import math

import jax
import jax.numpy as jnp
from jax import lax
from jax.experimental import pallas as pl
from jax.experimental.pallas import tpu as pltpu
from jax.sharding import PartitionSpec as P

HEAD_DIM = 128
HEADS = 4
CMP_BLOCK = 32
SEL_BLOCK = 64
TOPN = 16
WINDOW = 512
ROWS = 128
LANES = HEADS * ROWS

FAR = 1e30
RATE = HEAD_DIM**-0.5 * math.log2(math.e)
MESH = pl.DeviceIdType.MESH
F32 = jnp.float32
BF16 = jnp.bfloat16


def across(a, b):
    return lax.dot_general(a, b, (((1,), (1,)), ((), ())), preferred_element_type=F32)


def scores(k, q):
    return jnp.dot(jnp.concatenate([k, k], axis=1), q, preferred_element_type=F32)


def rows8(s):
    return s.reshape(s.shape[0] // 8, 8, s.shape[1])


def peak(parts, hides):
    tops = []
    for s, hide in zip(parts, hides):
        top = jnp.max(rows8(s), axis=0)
        tops.append(top if hide is None else top - hide)
    return jnp.max(functools.reduce(jnp.maximum, tops), axis=0, keepdims=True)


def weigh(parts, hides, top):
    packed, sums = [], []
    for s, hide in zip(parts, hides):
        w = jnp.exp2(s - (top if hide is None else top + hide))
        packed.append(w.astype(BF16))
        sums.append(jnp.sum(rows8(w), axis=0))
    total = jnp.sum(functools.reduce(jnp.add, sums), axis=0, keepdims=True)
    return jnp.concatenate(packed, axis=0), total


def times(vt, w):
    return jnp.dot(vt, w, preferred_element_type=F32)


def pipeline(fronts, backs):
    held = fronts[0]()
    for n, back in enumerate(backs):
        following = fronts[n + 1]() if n + 1 < len(fronts) else None
        back(*held)
        held = following


def merge_sort(keys):
    keys = list(keys)
    n = len(keys)
    p = 1
    while p < n:
        k = p
        while k >= 1:
            for j in range(k % p, n - k, 2 * k):
                for i in range(min(k, n - j - k)):
                    if (i + j) // (p * 2) == (i + j + k) // (p * 2):
                        lo, hi = keys[i + j], keys[i + j + k]
                        keys[i + j] = jnp.minimum(lo, hi)
                        keys[i + j + k] = jnp.maximum(lo, hi)
            k //= 2
        p *= 2
    return keys


def kernel(
    B,
    G,
    sel_in,
    queries_in,
    keys_in,
    values_in,
    key_in,
    key_out,
    value_in,
    value_out,
    positions_in,
    gate_weight_in,
    out,
    sel,
    queries,
    positions,
    gate_weight,
    w_in,
    w_out,
    shifted,
    sk,
    sv,
    pk,
    pv,
    ik,
    iv,
    stk,
    stv,
    cc,
    cvt,
    qs,
    wvt,
    pvt,
    fk,
    fvt,
    bias,
    wnear,
    acc,
    part,
    stat,
    gates,
    l_sem,
    w_sem,
    a_s,
    a_r,
    m_s,
    m_r,
    p_s,
    p_r,
    b_s,
    b_r,
    c_s,
    c_r,
    f_s,
    f_r,
    ready,
):
    T = queries.shape[0]
    N = T // CMP_BLOCK
    Y = G // 2
    STEPS = T // ROWS
    own_blocks = T // SEL_BLOCK
    per_row = G * own_blocks
    near_count = min(max(TOPN - (B - 1), 0), own_blocks)
    b = lax.axis_index("blk")
    g = lax.axis_index("grp")
    y = g // 2
    core = g % 2
    mate = g + 1 - 2 * core
    position = b * G + g
    first = position * T

    row = (sk, sv)
    prev = (pk, pv)
    staged = (stk, stv)
    inbox = (ik, iv)

    def slot(column):
        return pl.ds(column * own_blocks, own_blocks)

    def local(src, dst, sem):
        return pltpu.make_async_copy(src, dst, sem)

    def remote(src, dst, send, recv, dev):
        return pltpu.make_async_remote_copy(
            src_ref=src,
            dst_ref=dst,
            send_sem=send,
            recv_sem=recv,
            device_id=dev,
            device_id_type=MESH,
        )

    def at(stretch, column):
        return {"blk": stretch, "grp": column}

    def when(condition):
        return lambda body: pl.when(condition)(body)

    own_load = [
        local(keys_in, sk.at[slot(g)], l_sem.at[0]),
        local(values_in, sv.at[slot(g)], l_sem.at[1]),
    ]
    q_load = local(queries_in, queries, l_sem.at[2])
    gate_load = local(gate_weight_in, gate_weight, l_sem.at[3])
    shift_load = local(positions_in, positions, l_sem.at[4])
    sel_load = local(sel_in, sel, l_sem.at[5])
    weight_loads = [
        local(src, dst, w_sem.at[n])
        for n, (src, dst) in enumerate(
            (
                (key_in, w_in.at[0]),
                (value_in, w_in.at[1]),
                (key_out, w_out.at[0]),
                (value_out, w_out.at[1]),
            )
        )
    ]
    for load in own_load + [q_load, gate_load, shift_load, sel_load] + weight_loads:
        load.start()

    cc[...] = jnp.zeros_like(cc)
    pk[...] = jnp.zeros_like(pk)
    pv[...] = jnp.zeros_like(pv)

    source = jnp.logical_and(g == 1, b < B - 1)
    barrier = pltpu.get_barrier_semaphore()

    def greet(dev):
        pl.semaphore_signal(barrier, inc=1, device_id=dev, device_id_type=MESH)

    for e in range(1, G):
        greet(at(b, (g + e) % G))
    for d in range(1, B):

        @when(b + d < B)
        def _(d=d):
            greet(at(b + d, g))

    pl.semaphore_wait(barrier, G - 1 + b)

    def piece_of(column, h):
        return pl.ds(column * own_blocks + h * (own_blocks // 2), own_blocks // 2)

    def over_y(c, e, h):
        piece = row[c].at[piece_of(g, h)]
        dev = at(b, ((y + e) % Y) * 2 + core)
        return remote(piece, piece, a_s.at[c, e, h], a_r.at[c, e, h], dev)

    def to_mate(c, e, h):
        piece = row[c].at[piece_of(((y - e + Y) % Y) * 2 + core, h)]
        return remote(piece, piece, m_s.at[c, e, h], m_r.at[c, e, h], at(b, mate))

    def to_next(c, h):
        return remote(
            row[c].at[piece_of(G - 1, h)],
            prev[c].at[piece_of(0, h)],
            p_s.at[c, h],
            p_r.at[c, h],
            at((b + 1) % B, 0),
        )

    def block_out(c, d):
        return remote(
            staged[c].at[d - 1], inbox[c].at[b], b_s.at[c, d], b_r.at[c, d], at((b + d) % B, g)
        )

    mine_rows = pl.ds(pl.multiple_of((g * B + b) * N, N), N)

    def column_rows(column):
        return pl.ds(pl.multiple_of(column * B * N, N), B * N)

    def coarse_out(d):
        piece = cc.at[:, mine_rows, :]
        return remote(piece, piece, c_s.at[d], c_r.at[d], at((b + d) % B, g))

    def coarse_over_y(e):
        piece = cc.at[:, column_rows(g), :]
        dev = at(b, ((y + e) % Y) * 2 + core)
        return remote(piece, piece, f_s.at[0, e], f_r.at[0, e], dev)

    def coarse_to_mate(e):
        piece = cc.at[:, column_rows(((y - e + Y) % Y) * 2 + core), :]
        return remote(piece, piece, f_s.at[1, e], f_r.at[1, e], at(b, mate))

    halves = range(2)
    own_load[0].wait()
    for h in halves:
        for e in range(1, Y):
            over_y(0, e, h).start()
        to_mate(0, 0, h).start()
    own_load[1].wait()
    for h in halves:
        to_mate(1, 0, h).start()

    for d in range(1, B):

        @when(b - d >= 0)
        def _(d=d):
            pl.semaphore_signal(ready.at[d], inc=1, device_id=at(b - d, g), device_id_type=MESH)

    q_load.wait()
    for step in range(STEPS):
        for h in range(HEADS):
            piece = queries[step * ROWS : (step + 1) * ROWS, h * HEAD_DIM : (h + 1) * HEAD_DIM]
            piece = piece.T.astype(F32) * RATE
            high = piece.astype(BF16)
            qs[step, :HEAD_DIM, h * ROWS : (h + 1) * ROWS] = high
            qs[step, HEAD_DIM:, h * ROWS : (h + 1) * ROWS] = (piece - high.astype(F32)).astype(BF16)

    shift_load.wait()
    flat = (T, HEAD_DIM)
    for c in range(2):
        shift = positions[c].astype(F32)
        tokens = row[c][slot(g)].reshape(flat).astype(F32).reshape(N, CMP_BLOCK, HEAD_DIM)
        shifted[c] = (tokens + shift[None]).reshape(flat)
    wvt[...] = sv[slot(g)].reshape(flat).T
    for load in weight_loads:
        load.wait()
    for c in range(2):
        wide = jnp.concatenate(
            [shifted[c, pl.ds(t, N, stride=CMP_BLOCK), :].astype(BF16) for t in range(CMP_BLOCK)],
            axis=1,
        )
        hidden = jax.nn.silu(jnp.dot(wide, w_in[c], preferred_element_type=F32)).astype(BF16)
        mine = jnp.dot(hidden, w_out[c], preferred_element_type=F32).astype(BF16)
        cc[c, mine_rows, :] = mine
        cc[c, G * B * N : G * B * N + N, :] = mine
    for h in halves:
        for e in range(1, Y):
            over_y(1, e, h).start()

    def coarse_on(low, high):
        for d in range(low, high):

            @when(b + d < B)
            def _(d=d):
                pl.semaphore_wait(ready.at[d], 1)
                coarse_out(d).start()

    coarse_on(1, B // 2)

    def iotas(count):
        k = lax.broadcasted_iota(jnp.int32, (count, LANES), 0)
        q = lax.broadcasted_iota(jnp.int32, (count, LANES), 1) % ROWS
        return k, q

    def gate(n, step):
        cols = pl.ds(step * ROWS, ROWS)
        return jnp.concatenate(
            [gates[n * HEADS + h : n * HEADS + h + 1, cols] for h in range(HEADS)], axis=1
        )

    def keep(which, step, mixed, top, total):
        part[which, step] = mixed
        stat[which, step, 0:1] = top
        stat[which, step, 1:2] = total

    def join(which, step, mixed, total, best):
        old = jnp.exp2(stat[which, step, 0:1] - best)
        return part[which, step] * old + mixed, stat[which, step, 1:2] * old + total

    kd, qd = iotas(ROWS)
    own_keys = sk[slot(g)].reshape(flat)

    def own_front(step):
        count = (step + 1) * ROWS
        s = scores(own_keys[:count], qs[step])
        parts = [jnp.where(kd <= qd, s[count - ROWS :], -FAR)]
        if step > 0:
            parts = [s[: count - ROWS]] + parts
        hides = [None] * len(parts)
        return parts, hides, peak(parts, hides)

    def own_back(step, parts, hides, top):
        w, total = weigh(parts, hides, top)
        keep(0, step, times(wvt[:, : (step + 1) * ROWS], w), top, total)

    def spans(front, back):
        return (
            [functools.partial(front, step) for step in range(STEPS)],
            [functools.partial(back, step) for step in range(STEPS)],
        )

    pipeline(*spans(own_front, own_back))
    coarse_on(B // 2, B)

    def relay(c, h):
        for e in range(1, Y):
            over_y(c, e, h).wait_recv()
            to_mate(c, e, h).start()

        @when(source)
        def _():
            to_next(c, h).start()

    relay(0, 0)
    gate_load.wait()
    gates[...] = jax.nn.sigmoid(across(gate_weight[...], queries[...]))
    sel_load.wait()

    def owner_of(j):
        return lax.div(j, per_row)

    def same(left, right):
        gap = left - right
        return 1 - jnp.minimum(jnp.maximum(gap, -gap), 1)

    picks = []
    for d in range(1, B):
        line = jnp.minimum(b + d, B - 1) * G + g
        pick = jnp.int32(0)
        for i in range(TOPN):
            j = sel[i, line]
            pick = pick + same(owner_of(j), b) * (j - b * per_row)
        picks.append(pick)

    order = []
    for i in range(TOPN):
        j = sel[i, position]
        rel = j - b * per_row - g * own_blocks
        wrapped = jnp.where(rel < 0, rel + per_row, rel)
        order.append(jnp.where(j >= b * per_row, wrapped, j + per_row))
    order = merge_sort(order)

    def entry(i):
        code = order[i]
        near = code < per_row
        turned = code + g * own_blocks
        rank = jnp.where(turned >= per_row, turned - per_row, turned)
        rank = jnp.where(near, rank, 0)
        start = jnp.where(near, (b * per_row + rank) * SEL_BLOCK, 0)
        owner = jnp.where(near, 0, owner_of(code - per_row))
        return near, rank, owner, start

    def spread(c):
        for e in range(Y):
            for h in halves:
                to_mate(c, e, h).wait_recv()
        for d in range(B - 1, 0, -1):

            @when(b + d < B)
            def _(d=d):
                staged[c][d - 1] = row[c][picks[d - 1]]

        for d in range(B - 1, 0, -1):

            @when(b + d < B)
            def _(d=d):
                block_out(c, d).start()

    relay(0, 1)

    for d in range(1, B):

        @when(b - d >= 0)
        def _(d=d):
            coarse_out(d).wait_recv()

    for e in range(1, Y):
        coarse_over_y(e).start()
    coarse_to_mate(0).start()

    spread(0)

    entries = [entry(i) for i in range(TOPN)]
    for i in range(near_count):
        fk[pl.ds(i * SEL_BLOCK, SEL_BLOCK), :] = sk[entries[i][1]]

    ks, qf = iotas(SEL_BLOCK)
    ahead = ks - qf

    def fine_parts(step, low, high):
        s = scores(fk[pl.ds(low * SEL_BLOCK, (high - low) * SEL_BLOCK), :], qs[step])
        parts, hides = [], []
        for i in range(low, high):
            piece = s[(i - low) * SEL_BLOCK : (i - low + 1) * SEL_BLOCK]
            start = entries[i][3]
            if i < own_blocks:
                parts.append(jnp.where(ahead <= first + step * ROWS - start, piece, -FAR))
                hides.append(None)
            else:
                parts.append(piece)
                hides.append(jnp.where(start <= first, 0.0, FAR).astype(F32))
        return parts, hides

    def near_front(step):
        parts, hides = fine_parts(step, 0, near_count)
        return parts, hides, peak(parts, hides)

    def near_back(step, parts, hides, top):
        w, total = weigh(parts, hides, top)
        wnear[step] = w
        stat[1, step, 0:1] = top
        stat[1, step, 1:2] = total

    half = STEPS // 2
    if near_count > 0:
        near_fronts, near_backs = spans(near_front, near_back)
        pipeline(near_fronts[:half], near_backs[:half])
    relay(1, 0)
    if near_count > 0:
        pipeline(near_fronts[half:], near_backs[half:])
    relay(1, 1)
    spread(1)

    if near_count > 0:
        for i in range(near_count):
            fvt[:, pl.ds(i * SEL_BLOCK, SEL_BLOCK)] = sv[entries[i][1]].T
        for step in range(STEPS):
            part[1, step] = times(fvt[:, : near_count * SEL_BLOCK], wnear[step])

    for e in range(1, Y):
        coarse_over_y(e).wait_recv()
        coarse_to_mate(e).start()

    def prev_phase(prev_keys, opening):
        def prev_front(step):
            s = scores(prev_keys[step * ROWS :], qs[step])
            parts = [jnp.where(kd > qd, s[:ROWS], -FAR)]
            if step < STEPS - 1:
                parts.append(s[ROWS:])
            hides = [opening] * len(parts)
            return parts, hides, jnp.maximum(peak(parts, hides), stat[0, step, 0:1])

        def prev_back(step, parts, hides, top):
            w, total = weigh(parts, hides, top)
            mixed = times(pvt[:, step * ROWS :], w)
            mixed, total = join(0, step, mixed, total, top)
            part[0, step] = mixed * (gate(2, step) / total)

        pipeline(*spans(prev_front, prev_back))

    @when(g > 0)
    def _():
        before = slot(jnp.maximum(g - 1, 0))
        pvt[...] = sv[before].reshape(flat).T
        prev_phase(sk[before].reshape(flat), None)

    for e in range(Y):
        coarse_to_mate(e).wait_recv()

    coarse_count = G * B * N
    cvt[...] = cc[1].T
    k = lax.broadcasted_iota(jnp.int32, (coarse_count, ROWS), 0)
    seen = ((k // N) % B) * G + k // (B * N) < position
    bias[...] = jnp.where(seen, 0.0, -FAR)
    kc, qc = iotas(N)
    ends = kc * CMP_BLOCK + (CMP_BLOCK - 1) - qc

    def coarse_front(step):
        s = scores(cc[0, : coarse_count + N, :], qs[step])
        parts = [
            s[:coarse_count] + jnp.concatenate([bias[...]] * HEADS, axis=1),
            jnp.where(ends <= step * ROWS, s[coarse_count:], -FAR),
        ]
        hides = [None] * len(parts)
        return parts, hides, jnp.maximum(peak(parts, hides), 0.0)

    def coarse_back(step, parts, hides, top):
        w, total = weigh(parts, hides, top)
        w = jnp.concatenate([w, jnp.zeros((ROWS - N, LANES), BF16)], axis=0)
        total = total + jnp.exp2(-top)
        acc[step] = times(cvt[...], w) * (gate(0, step) / total)

    pipeline(*spans(coarse_front, coarse_back))

    @when(g == 0)
    def _():
        @when(b > 0)
        def _():
            for c in range(2):
                for h in halves:
                    to_next(c, h).wait_recv()

        opening = jnp.where(b == 0, FAR, 0.0).astype(F32)
        pvt[...] = pv[...].reshape(flat).T
        prev_phase(pk[...].reshape(flat), opening)

    for c in range(2):
        for d in range(1, B):

            @when(b - d >= 0)
            def _(c=c, d=d):
                block_out(c, d).wait_recv()

    for i in range(near_count, TOPN):
        near, rank, owner, _ = entries[i]
        fk[pl.ds(i * SEL_BLOCK, SEL_BLOCK), :] = jnp.where(near, sk[rank], ik[owner])
        fvt[:, pl.ds(i * SEL_BLOCK, SEL_BLOCK)] = jnp.where(near, sv[rank], iv[owner]).T

    def far_front(step):
        parts, hides = fine_parts(step, near_count, TOPN)
        top = peak(parts, hides)
        if near_count > 0:
            top = jnp.maximum(top, stat[1, step, 0:1])
        return parts, hides, top

    def far_back(step, parts, hides, top):
        w, total = weigh(parts, hides, top)
        mixed = times(fvt[:, near_count * SEL_BLOCK :], w)
        if near_count > 0:
            mixed, total = join(1, step, mixed, total, top)
        mixed = (acc[step] + part[0, step] + mixed * (gate(1, step) / total)).astype(BF16)
        for h in range(HEADS):
            out[step * ROWS : (step + 1) * ROWS, h * HEAD_DIM : (h + 1) * HEAD_DIM] = mixed[
                :, h * ROWS : (h + 1) * ROWS
            ].T

    pipeline(*spans(far_front, far_back))

    for c in range(2):
        for h in halves:
            for e in range(1, Y):
                over_y(c, e, h).wait_send()
            for e in range(Y):
                to_mate(c, e, h).wait_send()

        @when(source)
        def _(c=c):
            for h in halves:
                to_next(c, h).wait_send()

        for d in range(1, B):

            @when(b + d < B)
            def _(c=c, d=d):
                block_out(c, d).wait_send()

    for d in range(1, B):

        @when(b + d < B)
        def _(d=d):
            coarse_out(d).wait_send()

    for e in range(1, Y):
        coarse_over_y(e).wait_send()
    for e in range(Y):
        coarse_to_mate(e).wait_send()


def per_device(
    queries, keys, values, selected, key_in, key_out, value_in, value_out, positions, gate_weight
):
    B = lax.axis_size("blk")
    G = lax.axis_size("grp")
    T = keys.shape[0]
    N = T // CMP_BLOCK
    Y = G // 2
    STEPS = T // ROWS
    own_blocks = T // SEL_BLOCK
    inner, hidden = key_in.shape
    near_keys = min(max(TOPN - (B - 1), 0), own_blocks) * SEL_BLOCK
    anywhere = pl.BlockSpec(memory_space=pl.ANY)
    dma = pltpu.SemaphoreType.DMA
    regular = pltpu.SemaphoreType.REGULAR

    def buf(*shape, dtype=BF16):
        return pltpu.VMEM(shape, dtype)

    def blocks(count):
        return buf(count, SEL_BLOCK, HEAD_DIM)

    return pl.pallas_call(
        functools.partial(kernel, B, G),
        out_shape=pltpu.VMEM(queries.shape, BF16),
        in_specs=[anywhere] * 10,
        out_specs=pl.BlockSpec(memory_space=pltpu.VMEM),
        scratch_shapes=[
            pltpu.SMEM((TOPN, B * G), jnp.int32),
            buf(*queries.shape),
            buf(*positions.shape),
            buf(gate_weight.shape[1], gate_weight.shape[0]),
            buf(2, inner, hidden),
            buf(2, hidden, HEAD_DIM),
            buf(2, T, HEAD_DIM, dtype=F32),
            blocks(G * own_blocks),
            blocks(G * own_blocks),
            blocks(own_blocks),
            blocks(own_blocks),
            blocks(B),
            blocks(B),
            blocks(B - 1),
            blocks(B - 1),
            buf(2, G * B * N + ROWS, HEAD_DIM),
            buf(HEAD_DIM, G * B * N + ROWS),
            buf(STEPS, 2 * HEAD_DIM, LANES),
            buf(HEAD_DIM, T),
            buf(HEAD_DIM, T),
            buf(TOPN * SEL_BLOCK, HEAD_DIM),
            buf(HEAD_DIM, TOPN * SEL_BLOCK),
            buf(G * B * N, ROWS, dtype=F32),
            buf(STEPS, max(near_keys, SEL_BLOCK), LANES),
            buf(STEPS, HEAD_DIM, LANES, dtype=F32),
            buf(2, STEPS, HEAD_DIM, LANES, dtype=F32),
            buf(2, STEPS, 8, LANES, dtype=F32),
            buf(3 * HEADS, T, dtype=F32),
            dma((6,)),
            dma((4,)),
            dma((2, Y, 2)),
            dma((2, Y, 2)),
            dma((2, Y, 2)),
            dma((2, Y, 2)),
            dma((2, 2)),
            dma((2, 2)),
            dma((2, B)),
            dma((2, B)),
            dma((B,)),
            dma((B,)),
            dma((2, Y)),
            dma((2, Y)),
            regular((B,)),
        ],
        compiler_params=pltpu.CompilerParams(
            collective_id=0, has_side_effects=True, vmem_limit_bytes=56 << 20
        ),
    )(
        selected.T,
        queries,
        keys.reshape(T // SEL_BLOCK, SEL_BLOCK, HEAD_DIM),
        values.reshape(T // SEL_BLOCK, SEL_BLOCK, HEAD_DIM),
        key_in,
        key_out,
        value_in,
        value_out,
        positions,
        gate_weight.T,
    )


def solution(mesh):
    rows = P(("blk", "grp"), None)
    return jax.shard_map(
        per_device,
        mesh=mesh,
        in_specs=(rows, rows, rows, P(), P(), P(), P(), P(), P(), P()),
        out_specs=rows,
        check_vma=False,
    )
```

```python
import functools
import math

import jax
import jax.numpy as jnp
from jax import lax
from jax.experimental import pallas as pl
from jax.experimental.pallas import tpu as pltpu
from jax.sharding import PartitionSpec as P

HEAD_DIM = 128
HEADS = 4
TALL = HEAD_DIM + 16
CMP_BLOCK = 32
SEL_BLOCK = 64
TOPN = 16
WINDOW = 512
ROWS = 128
LANES = HEADS * ROWS

FAR = 1e30
RATE = HEAD_DIM**-0.5 * math.log2(math.e)
MESH = pl.DeviceIdType.MESH
F32 = jnp.float32
BF16 = jnp.bfloat16


def across(a, b):
    return lax.dot_general(a, b, (((1,), (1,)), ((), ())), preferred_element_type=F32)


def scores(k, q):
    return jnp.dot(jnp.concatenate([k, k], axis=1), q, preferred_element_type=F32)


def rows8(s):
    return s.reshape(s.shape[0] // 8, 8, s.shape[1])


def peak(parts, hides):
    tops = []
    for s, hide in zip(parts, hides):
        top = jnp.max(rows8(s), axis=0)
        tops.append(top if hide is None else top - hide)
    return jnp.max(functools.reduce(jnp.maximum, tops), axis=0, keepdims=True)


def weigh(parts, hides, top):
    packed = []
    for s, hide in zip(parts, hides):
        w = jnp.exp2(s - (top if hide is None else top + hide))
        packed.append(w.astype(BF16))
    return jnp.concatenate(packed, axis=0)


def times(vt, w):
    both = jnp.dot(vt, w, preferred_element_type=F32)
    return both[:HEAD_DIM], both[HEAD_DIM : HEAD_DIM + 1]


def pipeline(fronts, backs):
    held = fronts[0]()
    for n, back in enumerate(backs):
        following = fronts[n + 1]() if n + 1 < len(fronts) else None
        back(*held)
        held = following


def merge_sort(keys):
    keys = list(keys)
    n = len(keys)
    p = 1
    while p < n:
        k = p
        while k >= 1:
            for j in range(k % p, n - k, 2 * k):
                for i in range(min(k, n - j - k)):
                    if (i + j) // (p * 2) == (i + j + k) // (p * 2):
                        lo, hi = keys[i + j], keys[i + j + k]
                        keys[i + j] = jnp.minimum(lo, hi)
                        keys[i + j + k] = jnp.maximum(lo, hi)
            k //= 2
        p *= 2
    return keys


def kernel(
    B,
    G,
    sel_in,
    queries_in,
    keys_in,
    values_in,
    key_in,
    key_out,
    value_in,
    value_out,
    positions_in,
    gate_weight_in,
    out,
    sel,
    queries,
    positions,
    gate_weight,
    w_in,
    w_out,
    shifted,
    sk,
    sv,
    pk,
    pv,
    ik,
    iv,
    stk,
    stv,
    cc,
    cvt,
    cvt_far,
    qs,
    wvt,
    pvt,
    fk,
    fvt,
    bias,
    wnear,
    acc,
    part,
    stat,
    gates,
    l_sem,
    w_sem,
    a_s,
    a_r,
    m_s,
    m_r,
    p_s,
    p_r,
    b_s,
    b_r,
    c_s,
    c_r,
    f_s,
    f_r,
    ready,
):
    T = queries.shape[0]
    N = T // CMP_BLOCK
    Y = G // 2
    STEPS = T // ROWS
    own_blocks = T // SEL_BLOCK
    per_row = G * own_blocks
    near_count = min(max(TOPN - (B - 1), 0), own_blocks)
    b = lax.axis_index("blk")
    g = lax.axis_index("grp")
    y = g // 2
    core = g % 2
    mate = g + 1 - 2 * core
    position = b * G + g
    first = position * T

    row = (sk, sv)
    prev = (pk, pv)
    staged = (stk, stv)
    inbox = (ik, iv)

    flat = (T, HEAD_DIM)

    def slot(column):
        return pl.ds(column * own_blocks, own_blocks)

    def local(src, dst, sem):
        return pltpu.make_async_copy(src, dst, sem)

    def remote(src, dst, send, recv, dev):
        return pltpu.make_async_remote_copy(
            src_ref=src,
            dst_ref=dst,
            send_sem=send,
            recv_sem=recv,
            device_id=dev,
            device_id_type=MESH,
        )

    def at(stretch, column):
        return {"blk": stretch, "grp": column}

    def when(condition):
        return lambda body: pl.when(condition)(body)

    own_load = [
        local(keys_in, sk.at[slot(g)], l_sem.at[0]),
        local(values_in, sv.at[slot(g)], l_sem.at[1]),
    ]
    q_load = local(queries_in, queries, l_sem.at[2])
    gate_load = local(gate_weight_in, gate_weight, l_sem.at[3])
    shift_load = local(positions_in, positions, l_sem.at[4])
    sel_load = local(sel_in, sel, l_sem.at[5])
    weight_loads = [
        local(src, dst, w_sem.at[n])
        for n, (src, dst) in enumerate(
            (
                (key_in, w_in.at[0]),
                (value_in, w_in.at[1]),
                (key_out, w_out.at[0]),
                (value_out, w_out.at[1]),
            )
        )
    ]
    for load in own_load + [q_load, shift_load] + weight_loads[0::2] + [gate_load, sel_load]:
        load.start()

    cc[...] = jnp.zeros_like(cc)

    source = jnp.logical_and(g == G - 1, b < B - 1)
    crossed = jnp.logical_and(g == 1, b < B - 1)
    bridge = jnp.logical_and(g == G - 2, b > 0)
    barrier = pltpu.get_barrier_semaphore()

    def greet(dev):
        pl.semaphore_signal(barrier, inc=1, device_id=dev, device_id_type=MESH)

    for e in range(1, G):
        greet(at(b, (g + e) % G))
    for d in range(1, B):

        @when(b + d < B)
        def _(d=d):
            greet(at(b + d, g))

    for load in own_load:
        load.wait()
    for load in weight_loads[1::2]:
        load.start()
    mine_rows = pl.ds(pl.multiple_of((g * B + b) * N, N), N)

    def compress(c):
        shift = positions[c].astype(F32)
        tokens = row[c][slot(g)].reshape(flat).astype(F32).reshape(N, CMP_BLOCK, HEAD_DIM)
        shifted[c] = (tokens + shift[None]).reshape(flat)
        for load in weight_loads[c::2]:
            load.wait()
        wide = jnp.concatenate(
            [shifted[c, pl.ds(t, N, stride=CMP_BLOCK), :].astype(BF16) for t in range(CMP_BLOCK)],
            axis=1,
        )
        hidden = jax.nn.silu(jnp.dot(wide, w_in[c], preferred_element_type=F32)).astype(BF16)
        mine = jnp.dot(hidden, w_out[c], preferred_element_type=F32).astype(BF16)
        cc[c, mine_rows, :] = mine
        cc[c, G * B * N : G * B * N + N, :] = mine

    shift_load.wait()

    early = jnp.logical_and(b == 0, y == 0)
    late = jnp.logical_or(b > 0, y > 0)

    @when(early)
    def _():
        compress(0)
        compress(1)

    pl.semaphore_wait(barrier, G - 1 + b)

    def piece_of(column, h):
        return pl.ds(column * own_blocks + h * (own_blocks // 2), own_blocks // 2)

    def over_y(c, e, h):
        piece = row[c].at[piece_of(g, h)]
        dev = at(b, ((y + e) % Y) * 2 + core)
        return remote(piece, piece, a_s.at[c, e, h], a_r.at[c, e, h], dev)

    def to_mate(c, e, h):
        piece = row[c].at[piece_of(((y - e + Y) % Y) * 2 + core, h)]
        return remote(piece, piece, m_s.at[c, e, h], m_r.at[c, e, h], at(b, mate))

    def keys_on():
        return remote(sk.at[slot(G - 1)], pk, p_s.at[0], p_r.at[0], at((b + 1) % B, 0))

    def values_on():
        return remote(sv.at[slot(G - 1)], pv, p_s.at[1], p_r.at[1], at((b + 1) % B, G - 2))

    def values_over():
        return remote(pv, pv, p_s.at[2], p_r.at[2], at(b, 0))

    def block_out(c, d):
        return remote(
            staged[c].at[d - 1], inbox[c].at[b], b_s.at[c, d], b_r.at[c, d], at((b + d) % B, g)
        )

    def column_rows(column):
        return pl.ds(pl.multiple_of(column * B * N, N), B * N)

    def coarse_out(d):
        piece = cc.at[:, mine_rows, :]
        return remote(piece, piece, c_s.at[d], c_r.at[d], at((b + d) % B, g))

    def coarse_over_y(e):
        piece = cc.at[:, column_rows(g), :]
        dev = at(b, ((y + e) % Y) * 2 + core)
        return remote(piece, piece, f_s.at[0, e], f_r.at[0, e], dev)

    def coarse_to_mate(e):
        piece = cc.at[:, column_rows(((y - e + Y) % Y) * 2 + core), :]
        return remote(piece, piece, f_s.at[1, e], f_r.at[1, e], at(b, mate))

    halves = range(2)
    for h in halves:
        for e in range(1, Y):
            over_y(0, e, h).start()
        to_mate(0, 0, h).start()
    for h in halves:
        to_mate(1, 0, h).start()

    for d in range(1, B):

        @when(b - d >= 0)
        def _(d=d):
            pl.semaphore_signal(ready.at[d], inc=1, device_id=at(b - d, g), device_id_type=MESH)

    q_load.wait()
    for step in range(STEPS):
        for h in range(HEADS):
            piece = queries[step * ROWS : (step + 1) * ROWS, h * HEAD_DIM : (h + 1) * HEAD_DIM]
            piece = piece.T.astype(F32) * RATE
            high = piece.astype(BF16)
            qs[step, :HEAD_DIM, h * ROWS : (h + 1) * ROWS] = high
            qs[step, HEAD_DIM:, h * ROWS : (h + 1) * ROWS] = (piece - high.astype(F32)).astype(BF16)

    for turned in (wvt, pvt, cvt, cvt_far, fvt):
        turned[HEAD_DIM:, :] = jnp.ones_like(turned[HEAD_DIM:, :])
    wvt[:HEAD_DIM] = sv[slot(g)].reshape(flat).T

    def iotas(count):
        k = lax.broadcasted_iota(jnp.int32, (count, LANES), 0)
        q = lax.broadcasted_iota(jnp.int32, (count, LANES), 1) % ROWS
        return k, q

    def gate(n, step):
        cols = pl.ds(step * ROWS, ROWS)
        return jnp.concatenate(
            [gates[n * HEADS + h : n * HEADS + h + 1, cols] for h in range(HEADS)], axis=1
        )

    def keep(which, step, top, mixed, total):
        part[which, step] = mixed
        stat[which, step, 0:1] = top
        stat[which, step, 1:2] = total

    def join(which, step, best, mixed, total):
        old = jnp.exp2(stat[which, step, 0:1] - best)
        return part[which, step] * old + mixed, stat[which, step, 1:2] * old + total

    @when(late)
    def _():
        compress(0)

    for h in halves:
        for e in range(1, Y):
            over_y(1, e, h).start()

    @when(source)
    def _():
        pl.semaphore_wait(ready.at[1], 1)
        values_on().start()

    @when(late)
    def _():
        compress(1)

    def coarse_on(low, high, which=True):
        for d in range(low, high):

            @when(jnp.logical_and(b + d < B, which))
            def _(d=d):
                if d == 1:

                    @when(g < G - 1)
                    def _():
                        pl.semaphore_wait(ready.at[d], 1)
                else:
                    pl.semaphore_wait(ready.at[d], 1)
                coarse_out(d).start()

    coarse_on(1, B // 2, late)

    gate_load.wait()
    gates[...] = jax.nn.sigmoid(across(gate_weight[...], queries[...]))
    sel_load.wait()

    def owner_of(j):
        return lax.div(j, per_row)

    def same(left, right):
        gap = left - right
        return 1 - jnp.minimum(jnp.maximum(gap, -gap), 1)

    picks = []
    for d in range(1, B):
        line = jnp.minimum(b + d, B - 1) * G + g
        pick = jnp.int32(0)
        for i in range(TOPN):
            j = sel[i, line]
            pick = pick + same(owner_of(j), b) * (j - b * per_row)
        picks.append(pick)

    order = []
    for i in range(TOPN):
        j = sel[i, position]
        rel = j - b * per_row - g * own_blocks
        wrapped = jnp.where(rel < 0, rel + per_row, rel)
        order.append(jnp.where(j >= b * per_row, wrapped, j + per_row))
    order = merge_sort(order)

    def entry(i):
        code = order[i]
        near = code < per_row
        turned = code + g * own_blocks
        rank = jnp.where(turned >= per_row, turned - per_row, turned)
        rank = jnp.where(near, rank, 0)
        start = jnp.where(near, (b * per_row + rank) * SEL_BLOCK, 0)
        owner = jnp.where(near, 0, owner_of(code - per_row))
        return near, rank, owner, start

    kd, qd = iotas(ROWS)
    own_keys = sk[slot(g)].reshape(flat)

    def own_front(step):
        count = (step + 1) * ROWS
        s = scores(own_keys[:count], qs[step])
        parts = [jnp.where(kd <= qd, s[count - ROWS :], -FAR)]
        if step > 0:
            parts = [s[: count - ROWS]] + parts
        hides = [None] * len(parts)
        return parts, hides, peak(parts, hides)

    def own_back(step, parts, hides, top):
        w = weigh(parts, hides, top)
        keep(0, step, top, *times(wvt[:, : (step + 1) * ROWS], w))

    def spans(front, back):
        return (
            [functools.partial(front, step) for step in range(STEPS)],
            [functools.partial(back, step) for step in range(STEPS)],
        )

    pipeline(*spans(own_front, own_back))
    coarse_on(1, B // 2, early)
    coarse_on(B // 2, B)

    def relay(c, h):
        for e in range(1, Y):
            over_y(c, e, h).wait_recv()
            to_mate(c, e, h).start()

    relay(0, 0)
    def spread(c):
        for e in range(1, Y):
            for h in halves:
                to_mate(c, e, h).wait_recv()
        for d in range(B - 1, 0, -1):

            @when(b + d < B)
            def _(d=d):
                staged[c][d - 1] = row[c][picks[d - 1]]

        for d in range(B - 1, 0, -1):

            @when(b + d < B)
            def _(d=d):
                block_out(c, d).start()

    relay(0, 1)

    @when(crossed)
    def _():
        keys_on().start()

    for c in range(2):
        for h in halves:
            to_mate(c, 0, h).wait_recv()

    def prev_phase(prev_keys):
        def prev_front(step):
            s = scores(prev_keys[step * ROWS :], qs[step])
            parts = [jnp.where(kd > qd, s[:ROWS], -FAR)]
            if step < STEPS - 1:
                parts.append(s[ROWS:])
            hides = [None] * len(parts)
            return parts, hides, jnp.maximum(peak(parts, hides), stat[0, step, 0:1])

        def prev_back(step, parts, hides, top):
            w = weigh(parts, hides, top)
            mixed, total = join(0, step, top, *times(pvt[:, step * ROWS :], w))
            part[0, step] = mixed * (gate(2, step) / total)

        pipeline(*spans(prev_front, prev_back))

    def prev_before():
        before = slot((g + G - 1) % G)
        pvt[:HEAD_DIM] = sv[before].reshape(flat).T
        prev_phase(sk[before].reshape(flat))

    @when(core == 1)
    def _():
        prev_before()

    def coarse_gather():
        for d in range(1, B):

            @when(b - d >= 0)
            def _(d=d):
                coarse_out(d).wait_recv()

        for e in range(1, Y):
            coarse_over_y(e).start()
        coarse_to_mate(0).start()

    spread(0)

    entries = [entry(i) for i in range(TOPN)]
    for i in range(near_count):
        fk[pl.ds(i * SEL_BLOCK, SEL_BLOCK), :] = sk[entries[i][1]]

    ks, qf = iotas(SEL_BLOCK)
    ahead = ks - qf

    def fine_parts(step, low, high):
        s = scores(fk[pl.ds(low * SEL_BLOCK, (high - low) * SEL_BLOCK), :], qs[step])
        parts, hides = [], []
        for i in range(low, high):
            piece = s[(i - low) * SEL_BLOCK : (i - low + 1) * SEL_BLOCK]
            start = entries[i][3]
            if i < own_blocks:
                parts.append(jnp.where(ahead <= first + step * ROWS - start, piece, -FAR))
                hides.append(None)
            else:
                parts.append(piece)
                hides.append(jnp.where(start <= first, 0.0, FAR).astype(F32))
        return parts, hides

    def near_front(step):
        parts, hides = fine_parts(step, 0, near_count)
        return parts, hides, peak(parts, hides)

    def near_back(step, parts, hides, top):
        wnear[step] = weigh(parts, hides, top)
        stat[1, step, 0:1] = top

    @when(core == 1)
    def _():
        relay(1, 0)
        coarse_gather()

    half = STEPS // 2
    if near_count > 0:
        near_fronts, near_backs = spans(near_front, near_back)
        pipeline(near_fronts[:half], near_backs[:half])
    @when(core == 0)
    def _():
        relay(1, 0)
        coarse_gather()

    @when(bridge)
    def _():
        values_on().wait_recv()
        values_over().start()

    @when(core == 1)
    def _():
        relay(1, 1)

    if near_count > 0:
        pipeline(near_fronts[half:], near_backs[half:])

    chip = 2 * B * N

    def chip_rows(e):
        return pl.ds(pl.multiple_of(((y + e) % Y) * chip, chip), chip)

    k = lax.broadcasted_iota(jnp.int32, (chip, ROWS), 0)
    for e in range(Y):
        column = ((y + e) % Y) * 2 + k // (B * N)
        seen = (k % (B * N)) // N * G + column < position
        bias[pl.ds(e * chip, chip), :] = jnp.where(seen, 0.0, -FAR)

    def coarse_phase():
        kc, qc = iotas(N)
        ends = kc * CMP_BLOCK + (CMP_BLOCK - 1) - qc
        mine = pl.ds(G * B * N, N)
        coarse_to_mate(0).wait_recv()
        cvt[:HEAD_DIM, :chip] = cc[1, chip_rows(0), :].T
        cvt[:HEAD_DIM, chip:] = cc[1, pl.ds(G * B * N, ROWS), :].T

        def coarse_front(step):
            k = jnp.concatenate([cc[0, chip_rows(0), :], cc[0, mine, :]], axis=0)
            s = scores(k, qs[step])
            parts = [
                s[:chip] + jnp.concatenate([bias[:chip, :]] * HEADS, axis=1),
                jnp.where(ends <= step * ROWS, s[chip:], -FAR),
            ]
            hides = [None] * len(parts)
            return parts, hides, jnp.maximum(peak(parts, hides), 0.0)

        def coarse_back(step, parts, hides, top):
            w = weigh(parts, hides, top)
            w = jnp.concatenate([w, jnp.zeros((ROWS - N, LANES), BF16)], axis=0)
            keep(2, step, top, *times(cvt[...], w))

        return spans(coarse_front, coarse_back)

    @when(core == 0)
    def _():
        relay(1, 1)
        pipeline(*coarse_phase())

    spread(1)

    if near_count > 0:
        for i in range(near_count):
            fvt[:HEAD_DIM, pl.ds(i * SEL_BLOCK, SEL_BLOCK)] = sv[entries[i][1]].T
        for step in range(STEPS):
            mixed, total = times(fvt[:, : near_count * SEL_BLOCK], wnear[step])
            part[1, step] = mixed
            stat[1, step, 1:2] = total

    def coarse_relay():
        for e in range(1, Y):
            coarse_over_y(e).wait_recv()
            coarse_to_mate(e).start()

    @when(core == 0)
    def _():
        coarse_relay()

    @when(core == 1)
    def _():
        fronts, backs = coarse_phase()
        pipeline(fronts[:half], backs[:half])
        coarse_relay()
        pipeline(fronts[half:], backs[half:])

    @when(jnp.logical_and(core == 0, g > 0))
    def _():
        prev_before()

    for e in range(1, Y):
        coarse_to_mate(e).wait_recv()

    cvt_far[:HEAD_DIM] = jnp.concatenate([cc[1, chip_rows(e), :] for e in range(1, Y)], axis=0).T

    def coarse_far_front(step):
        k = jnp.concatenate([cc[0, chip_rows(e), :] for e in range(1, Y)], axis=0)
        off = bias[pl.ds(chip, (Y - 1) * chip), :]
        parts = [scores(k, qs[step]) + jnp.concatenate([off] * HEADS, axis=1)]
        return parts, [None], jnp.maximum(peak(parts, [None]), stat[2, step, 0:1])

    def coarse_far_back(step, parts, hides, top):
        w = weigh(parts, hides, top)
        mixed, total = join(2, step, top, *times(cvt_far[...], w))
        acc[step] = mixed * (gate(0, step) / (total + jnp.exp2(-top)))

    pipeline(*spans(coarse_far_front, coarse_far_back))

    @when(jnp.logical_and(g == 0, b > 0))
    def _():
        keys_on().wait_recv()
        values_over().wait_recv()
        pvt[:HEAD_DIM] = pv[...].reshape(flat).T
        prev_phase(pk[...].reshape(flat))

    @when(position == 0)
    def _():
        for step in range(STEPS):
            part[0, step] = part[0, step] * (gate(2, step) / stat[0, step, 1:2])

    for c in range(2):
        for h in halves:
            for e in range(1, Y):
                over_y(c, e, h).wait_send()
            for e in range(Y):
                to_mate(c, e, h).wait_send()

    @when(source)
    def _():
        values_on().wait_send()

    @when(crossed)
    def _():
        keys_on().wait_send()

    @when(bridge)
    def _():
        values_over().wait_send()

    for d in range(1, B):

        @when(b + d < B)
        def _(d=d):
            coarse_out(d).wait_send()
            for c in range(2):
                block_out(c, d).wait_send()

    for e in range(1, Y):
        coarse_over_y(e).wait_send()
    for e in range(Y):
        coarse_to_mate(e).wait_send()

    for d in range(1, B):

        @when(b - d >= 0)
        def _(d=d):
            for c in range(2):
                block_out(c, d).wait_recv()

    for i in range(near_count, TOPN):
        near, rank, owner, _ = entries[i]
        fk[pl.ds(i * SEL_BLOCK, SEL_BLOCK), :] = jnp.where(near, sk[rank], ik[owner])
        fvt[:HEAD_DIM, pl.ds(i * SEL_BLOCK, SEL_BLOCK)] = jnp.where(near, sv[rank], iv[owner]).T

    def far_front(step):
        parts, hides = fine_parts(step, near_count, TOPN)
        top = peak(parts, hides)
        if near_count > 0:
            top = jnp.maximum(top, stat[1, step, 0:1])
        return parts, hides, top

    def far_back(step, parts, hides, top):
        w = weigh(parts, hides, top)
        mixed, total = times(fvt[:, near_count * SEL_BLOCK :], w)
        if near_count > 0:
            mixed, total = join(1, step, top, mixed, total)
        mixed = (acc[step] + part[0, step] + mixed * (gate(1, step) / total)).astype(BF16)
        for h in range(HEADS):
            out[step * ROWS : (step + 1) * ROWS, h * HEAD_DIM : (h + 1) * HEAD_DIM] = mixed[
                :, h * ROWS : (h + 1) * ROWS
            ].T

    pipeline(*spans(far_front, far_back))


def per_device(
    queries, keys, values, selected, key_in, key_out, value_in, value_out, positions, gate_weight
):
    B = lax.axis_size("blk")
    G = lax.axis_size("grp")
    T = keys.shape[0]
    N = T // CMP_BLOCK
    Y = G // 2
    STEPS = T // ROWS
    own_blocks = T // SEL_BLOCK
    inner, hidden = key_in.shape
    near_keys = min(max(TOPN - (B - 1), 0), own_blocks) * SEL_BLOCK
    anywhere = pl.BlockSpec(memory_space=pl.ANY)
    dma = pltpu.SemaphoreType.DMA
    regular = pltpu.SemaphoreType.REGULAR

    def buf(*shape, dtype=BF16):
        return pltpu.VMEM(shape, dtype)

    def blocks(count):
        return buf(count, SEL_BLOCK, HEAD_DIM)

    return pl.pallas_call(
        functools.partial(kernel, B, G),
        out_shape=pltpu.VMEM(queries.shape, BF16),
        in_specs=[anywhere] * 10,
        out_specs=pl.BlockSpec(memory_space=pltpu.VMEM),
        scratch_shapes=[
            pltpu.SMEM((TOPN, B * G), jnp.int32),
            buf(*queries.shape),
            buf(*positions.shape),
            buf(gate_weight.shape[1], gate_weight.shape[0]),
            buf(2, inner, hidden),
            buf(2, hidden, HEAD_DIM),
            buf(2, T, HEAD_DIM, dtype=F32),
            blocks(G * own_blocks),
            blocks(G * own_blocks),
            blocks(own_blocks),
            blocks(own_blocks),
            blocks(B),
            blocks(B),
            blocks(B - 1),
            blocks(B - 1),
            buf(2, G * B * N + ROWS, HEAD_DIM),
            buf(TALL, 2 * B * N + ROWS),
            buf(TALL, (Y - 1) * 2 * B * N),
            buf(STEPS, 2 * HEAD_DIM, LANES),
            buf(TALL, T),
            buf(TALL, T),
            buf(TOPN * SEL_BLOCK, HEAD_DIM),
            buf(TALL, TOPN * SEL_BLOCK),
            buf(G * B * N, ROWS, dtype=F32),
            buf(STEPS, max(near_keys, SEL_BLOCK), LANES),
            buf(STEPS, HEAD_DIM, LANES, dtype=F32),
            buf(3, STEPS, HEAD_DIM, LANES, dtype=F32),
            buf(3, STEPS, 8, LANES, dtype=F32),
            buf(3 * HEADS, T, dtype=F32),
            dma((6,)),
            dma((4,)),
            dma((2, Y, 2)),
            dma((2, Y, 2)),
            dma((2, Y, 2)),
            dma((2, Y, 2)),
            dma((3,)),
            dma((3,)),
            dma((2, B)),
            dma((2, B)),
            dma((B,)),
            dma((B,)),
            dma((2, Y)),
            dma((2, Y)),
            regular((B,)),
        ],
        compiler_params=pltpu.CompilerParams(
            collective_id=0, has_side_effects=True, vmem_limit_bytes=56 << 20
        ),
    )(
        selected.T,
        queries,
        keys.reshape(T // SEL_BLOCK, SEL_BLOCK, HEAD_DIM),
        values.reshape(T // SEL_BLOCK, SEL_BLOCK, HEAD_DIM),
        key_in,
        key_out,
        value_in,
        value_out,
        positions,
        gate_weight.T,
    )


def solution(mesh):
    rows = P(("blk", "grp"), None)
    return jax.shard_map(
        per_device,
        mesh=mesh,
        in_specs=(rows, rows, rows, P(), P(), P(), P(), P(), P(), P()),
        out_specs=rows,
        check_vma=False,
    )
```

```python
import functools
import math

import jax
import jax.numpy as jnp
from jax import lax
from jax.experimental import pallas as pl
from jax.experimental.pallas import tpu as pltpu
from jax.sharding import PartitionSpec as P

HEAD_DIM = 128
HEADS = 4
TALL = HEAD_DIM + 16
CMP_BLOCK = 32
SEL_BLOCK = 64
TOPN = 16
WINDOW = 512
ROWS = 128
LANES = HEADS * ROWS

FAR = 1e30
RATE = HEAD_DIM**-0.5 * math.log2(math.e)
MESH = pl.DeviceIdType.MESH
F32 = jnp.float32
BF16 = jnp.bfloat16


def across(a, b):
    return lax.dot_general(a, b, (((1,), (1,)), ((), ())), preferred_element_type=F32)


def scores(k, q):
    return jnp.dot(jnp.concatenate([k, k], axis=1), q, preferred_element_type=F32)


def rows8(s):
    return s.reshape(s.shape[0] // 8, 8, s.shape[1])


def peak(parts, hides):
    tops = []
    for s, hide in zip(parts, hides):
        top = jnp.max(rows8(s), axis=0)
        tops.append(top if hide is None else top - hide)
    return jnp.max(functools.reduce(jnp.maximum, tops), axis=0, keepdims=True)


def weigh(parts, hides, top):
    packed = []
    for s, hide in zip(parts, hides):
        w = jnp.exp2(s - (top if hide is None else top + hide))
        packed.append(w.astype(BF16))
    return jnp.concatenate(packed, axis=0)


def times(vt, w):
    both = jnp.dot(vt, w, preferred_element_type=F32)
    return both[:HEAD_DIM], both[HEAD_DIM : HEAD_DIM + 1]


def pipeline(fronts, backs):
    held = fronts[0]()
    for n, back in enumerate(backs):
        following = fronts[n + 1]() if n + 1 < len(fronts) else None
        back(*held)
        held = following


def merge_sort(keys):
    keys = list(keys)
    n = len(keys)
    p = 1
    while p < n:
        k = p
        while k >= 1:
            for j in range(k % p, n - k, 2 * k):
                for i in range(min(k, n - j - k)):
                    if (i + j) // (p * 2) == (i + j + k) // (p * 2):
                        lo, hi = keys[i + j], keys[i + j + k]
                        keys[i + j] = jnp.minimum(lo, hi)
                        keys[i + j + k] = jnp.maximum(lo, hi)
            k //= 2
        p *= 2
    return keys


def kernel(
    B,
    G,
    sel_in,
    queries_in,
    keys_in,
    values_in,
    key_in,
    key_out,
    value_in,
    value_out,
    positions_in,
    gate_weight_in,
    out,
    sel,
    queries,
    positions,
    gate_weight,
    w_in,
    w_out,
    shifted,
    sk,
    sv,
    pk,
    pv,
    ik,
    iv,
    stk,
    stv,
    cc,
    cvt,
    cvt_far,
    qs,
    wvt,
    pvt,
    fk,
    fv,
    fvt,
    bias,
    wnear,
    acc,
    part,
    stat,
    gates,
    l_sem,
    w_sem,
    a_s,
    a_r,
    m_s,
    m_r,
    p_s,
    p_r,
    b_s,
    b_r,
    c_s,
    c_r,
    f_s,
    f_r,
    ready,
):
    T = queries.shape[0]
    N = T // CMP_BLOCK
    Y = G // 2
    STEPS = T // ROWS
    own_blocks = T // SEL_BLOCK
    per_row = G * own_blocks
    near_count = min(max(TOPN - (B - 1), 0), own_blocks)
    b = lax.axis_index("blk")
    g = lax.axis_index("grp")
    y = g // 2
    core = g % 2
    mate = g + 1 - 2 * core
    position = b * G + g
    first = position * T

    row = (sk, sv)
    prev = (pk, pv)
    staged = (stk, stv)
    inbox = (ik, iv)

    flat = (T, HEAD_DIM)

    def slot(column):
        return pl.ds(column * own_blocks, own_blocks)

    def local(src, dst, sem):
        return pltpu.make_async_copy(src, dst, sem)

    def remote(src, dst, send, recv, dev):
        return pltpu.make_async_remote_copy(
            src_ref=src,
            dst_ref=dst,
            send_sem=send,
            recv_sem=recv,
            device_id=dev,
            device_id_type=MESH,
        )

    def at(stretch, column):
        return {"blk": stretch, "grp": column}

    def when(condition):
        return lambda body: pl.when(condition)(body)

    own_load = [
        local(keys_in, sk.at[slot(g)], l_sem.at[0]),
        local(values_in, sv.at[slot(g)], l_sem.at[1]),
    ]
    q_load = local(queries_in, queries, l_sem.at[2])
    gate_load = local(gate_weight_in, gate_weight, l_sem.at[3])
    shift_load = local(positions_in, positions, l_sem.at[4])
    sel_load = local(sel_in, sel, l_sem.at[5])
    weight_loads = [
        local(src, dst, w_sem.at[n])
        for n, (src, dst) in enumerate(
            (
                (key_in, w_in.at[0]),
                (value_in, w_in.at[1]),
                (key_out, w_out.at[0]),
                (value_out, w_out.at[1]),
            )
        )
    ]
    for load in own_load + [q_load, shift_load] + weight_loads[0::2] + [gate_load, sel_load]:
        load.start()

    cc[...] = jnp.zeros_like(cc)

    source = jnp.logical_and(g == G - 1, b < B - 1)
    crossed = jnp.logical_and(g == 1, b < B - 1)
    bridge = jnp.logical_and(g == G - 2, b > 0)
    barrier = pltpu.get_barrier_semaphore()

    def greet(dev):
        pl.semaphore_signal(barrier, inc=1, device_id=dev, device_id_type=MESH)

    for e in range(1, G):
        greet(at(b, (g + e) % G))
    for d in range(1, B):

        @when(b + d < B)
        def _(d=d):
            greet(at(b + d, g))

    for load in own_load:
        load.wait()
    for load in weight_loads[1::2]:
        load.start()
    mine_rows = pl.ds(pl.multiple_of((g * B + b) * N, N), N)

    def compress(c):
        shift = positions[c].astype(F32)
        tokens = row[c][slot(g)].reshape(flat).astype(F32).reshape(N, CMP_BLOCK, HEAD_DIM)
        shifted[c] = (tokens + shift[None]).reshape(flat)
        for load in weight_loads[c::2]:
            load.wait()
        wide = jnp.concatenate(
            [shifted[c, pl.ds(t, N, stride=CMP_BLOCK), :].astype(BF16) for t in range(CMP_BLOCK)],
            axis=1,
        )
        hidden = jax.nn.silu(jnp.dot(wide, w_in[c], preferred_element_type=F32)).astype(BF16)
        mine = jnp.dot(hidden, w_out[c], preferred_element_type=F32).astype(BF16)
        cc[c, mine_rows, :] = mine
        cc[c, G * B * N : G * B * N + N, :] = mine

    shift_load.wait()

    early = jnp.logical_and(b == 0, y == 0)
    late = jnp.logical_or(b > 0, y > 0)

    @when(early)
    def _():
        compress(0)
        compress(1)

    pl.semaphore_wait(barrier, G - 1 + b)

    def piece_of(column, h):
        return pl.ds(column * own_blocks + h * (own_blocks // 2), own_blocks // 2)

    def over_y(c, e, h):
        piece = row[c].at[piece_of(g, h)]
        dev = at(b, ((y + e) % Y) * 2 + core)
        return remote(piece, piece, a_s.at[c, e, h], a_r.at[c, e, h], dev)

    def to_mate(c, e, h):
        piece = row[c].at[piece_of(((y - e + Y) % Y) * 2 + core, h)]
        return remote(piece, piece, m_s.at[c, e, h], m_r.at[c, e, h], at(b, mate))

    def keys_on():
        return remote(sk.at[slot(G - 1)], pk, p_s.at[0], p_r.at[0], at((b + 1) % B, 0))

    def values_on():
        return remote(sv.at[slot(G - 1)], pv, p_s.at[1], p_r.at[1], at((b + 1) % B, G - 2))

    def values_over():
        return remote(pv, pv, p_s.at[2], p_r.at[2], at(b, 0))

    def block_out(c, d):
        return remote(
            staged[c].at[d - 1], inbox[c].at[b], b_s.at[c, d], b_r.at[c, d], at((b + d) % B, g)
        )

    chunks = 4 if B % 4 == 0 else 1

    def column_rows(column, k):
        count = B // chunks * N
        return pl.ds(pl.multiple_of(column * B * N + k * count, N), count)

    def each_chunk(body):
        for k in range(chunks):

            @when(b >= k * (B // chunks))
            def _(k=k):
                body(k)

    def coarse_out(d):
        piece = cc.at[:, mine_rows, :]
        return remote(piece, piece, c_s.at[d], c_r.at[d], at((b + d) % B, g))

    def coarse_over_y(e, k):
        piece = cc.at[:, column_rows(g, k), :]
        dev = at(b, ((y + e) % Y) * 2 + core)
        return remote(piece, piece, f_s.at[0, e, k], f_r.at[0, e, k], dev)

    def coarse_to_mate(e, k):
        piece = cc.at[:, column_rows(((y - e + Y) % Y) * 2 + core, k), :]
        return remote(piece, piece, f_s.at[1, e, k], f_r.at[1, e, k], at(b, mate))

    halves = range(2)
    for h in halves:
        for e in range(1, Y):
            over_y(0, e, h).start()
        to_mate(0, 0, h).start()
    for h in halves:
        to_mate(1, 0, h).start()

    for d in range(1, B):

        @when(b - d >= 0)
        def _(d=d):
            pl.semaphore_signal(ready.at[d], inc=1, device_id=at(b - d, g), device_id_type=MESH)

    q_load.wait()
    for step in range(STEPS):
        for h in range(HEADS):
            piece = queries[step * ROWS : (step + 1) * ROWS, h * HEAD_DIM : (h + 1) * HEAD_DIM]
            piece = piece.T.astype(F32) * RATE
            high = piece.astype(BF16)
            qs[step, :HEAD_DIM, h * ROWS : (h + 1) * ROWS] = high
            qs[step, HEAD_DIM:, h * ROWS : (h + 1) * ROWS] = (piece - high.astype(F32)).astype(BF16)

    for turned in (wvt, pvt, cvt, cvt_far, fvt):
        turned[HEAD_DIM:, :] = jnp.ones_like(turned[HEAD_DIM:, :])
    wvt[:HEAD_DIM] = sv[slot(g)].reshape(flat).T

    def iotas(count):
        k = lax.broadcasted_iota(jnp.int32, (count, LANES), 0)
        q = lax.broadcasted_iota(jnp.int32, (count, LANES), 1) % ROWS
        return k, q

    def gate(n, step):
        cols = pl.ds(step * ROWS, ROWS)
        return jnp.concatenate(
            [gates[n * HEADS + h : n * HEADS + h + 1, cols] for h in range(HEADS)], axis=1
        )

    def keep(which, step, top, mixed, total):
        part[which, step] = mixed
        stat[which, step, 0:1] = top
        stat[which, step, 1:2] = total

    def join(which, step, best, mixed, total):
        old = jnp.exp2(stat[which, step, 0:1] - best)
        return part[which, step] * old + mixed, stat[which, step, 1:2] * old + total

    @when(late)
    def _():
        compress(0)

    @when(source)
    def _():
        pl.semaphore_wait(ready.at[1], 1)
        values_on().start()

    @when(late)
    def _():
        compress(1)

    for h in halves:
        for e in range(1, Y):
            over_y(1, e, h).start()

    def coarse_on(low, high, which=True):
        for d in range(low, high):

            @when(jnp.logical_and(b + d < B, which))
            def _(d=d):
                if d == 1:

                    @when(g < G - 1)
                    def _():
                        pl.semaphore_wait(ready.at[d], 1)
                else:
                    pl.semaphore_wait(ready.at[d], 1)
                coarse_out(d).start()

    coarse_on(1, B // 2, late)

    gate_load.wait()
    gates[...] = jax.nn.sigmoid(across(gate_weight[...], queries[...]))
    sel_load.wait()

    def owner_of(j):
        return lax.div(j, per_row)

    def same(left, right):
        gap = left - right
        return 1 - jnp.minimum(jnp.maximum(gap, -gap), 1)

    picks = []
    for d in range(1, B):
        line = jnp.minimum(b + d, B - 1) * G + g
        pick = jnp.int32(0)
        for i in range(TOPN):
            j = sel[i, line]
            pick = pick + same(owner_of(j), b) * (j - b * per_row)
        picks.append(pick)

    order = []
    for i in range(TOPN):
        j = sel[i, position]
        rel = j - b * per_row - g * own_blocks
        wrapped = jnp.where(rel < 0, rel + per_row, rel)
        order.append(jnp.where(j >= b * per_row, wrapped, j + per_row))
    order = merge_sort(order)

    def entry(i):
        code = order[i]
        near = code < per_row
        turned = code + g * own_blocks
        rank = jnp.where(turned >= per_row, turned - per_row, turned)
        rank = jnp.where(near, rank, 0)
        start = jnp.where(near, (b * per_row + rank) * SEL_BLOCK, 0)
        owner = jnp.where(near, 0, owner_of(code - per_row))
        return near, rank, owner, start

    kd, qd = iotas(ROWS)
    own_keys = sk[slot(g)].reshape(flat)

    def own_front(step):
        count = (step + 1) * ROWS
        s = scores(own_keys[:count], qs[step])
        parts = [jnp.where(kd <= qd, s[count - ROWS :], -FAR)]
        if step > 0:
            parts = [s[: count - ROWS]] + parts
        hides = [None] * len(parts)
        return parts, hides, peak(parts, hides)

    def own_back(step, parts, hides, top):
        w = weigh(parts, hides, top)
        keep(0, step, top, *times(wvt[:, : (step + 1) * ROWS], w))

    def spans(front, back):
        return (
            [functools.partial(front, step) for step in range(STEPS)],
            [functools.partial(back, step) for step in range(STEPS)],
        )

    pipeline(*spans(own_front, own_back))
    coarse_on(1, B // 2, early)
    coarse_on(B // 2, B)

    def relay(c, h):
        for e in range(1, Y):
            over_y(c, e, h).wait_recv()
            to_mate(c, e, h).start()

    relay(0, 0)
    def spread(c):
        for e in range(1, Y):
            for h in halves:
                to_mate(c, e, h).wait_recv()
        for d in range(1, B):

            @when(b + d < B)
            def _(d=d):
                staged[c][d - 1] = row[c][picks[d - 1]]

        for d in range(1, B):

            @when(b + d < B)
            def _(d=d):
                block_out(c, d).start()

    relay(0, 1)

    @when(crossed)
    def _():
        keys_on().start()

    for c in range(2):
        for h in halves:
            to_mate(c, 0, h).wait_recv()

    def prev_front(prev_keys, step):
        s = scores(prev_keys[step * ROWS :], qs[step])
        parts = [jnp.where(kd > qd, s[:ROWS], -FAR)]
        if step < STEPS - 1:
            parts.append(s[ROWS:])
        hides = [None] * len(parts)
        return parts, hides, jnp.maximum(peak(parts, hides), stat[0, step, 0:1])

    def prev_phase(prev_keys):
        def back(step, parts, hides, top):
            w = weigh(parts, hides, top)
            mixed, total = join(0, step, top, *times(pvt[:, step * ROWS :], w))
            part[0, step] = mixed * (gate(2, step) / total)

        fronts = [functools.partial(prev_front, prev_keys, step) for step in range(STEPS)]
        pipeline(fronts, [functools.partial(back, step) for step in range(STEPS)])

    def prev_weights(prev_keys):
        fronts = [functools.partial(prev_front, prev_keys, step) for step in range(STEPS)]

        def back(step, parts, hides, top):
            wnear[step, : T - step * ROWS] = weigh(parts, hides, top)
            stat[0, step, 2:3] = top

        pipeline(fronts, [functools.partial(back, step) for step in range(STEPS)])

    def prev_product():
        for step in range(STEPS):
            both = times(pvt[:, step * ROWS :], wnear[step, : T - step * ROWS])
            mixed, total = join(0, step, stat[0, step, 2:3], *both)
            part[0, step] = mixed * (gate(2, step) / total)

    def prev_before():
        before = slot((g + G - 1) % G)
        pvt[:HEAD_DIM] = sv[before].reshape(flat).T
        prev_phase(sk[before].reshape(flat))

    @when(core == 1)
    def _():
        prev_before()

    def coarse_gather():
        for d in range(1, B):

            @when(b - d >= 0)
            def _(d=d):
                coarse_out(d).wait_recv()

        def send(k):
            for e in range(1, Y):
                coarse_over_y(e, k).start()
            coarse_to_mate(0, k).start()

        each_chunk(send)

    spread(0)

    entries = [entry(i) for i in range(TOPN)]
    for i in range(near_count):
        fk[pl.ds(i * SEL_BLOCK, SEL_BLOCK), :] = sk[entries[i][1]]

    ks, qf = iotas(SEL_BLOCK)
    ahead = ks - qf

    def fine_parts(step, low, high):
        s = scores(fk[pl.ds(low * SEL_BLOCK, (high - low) * SEL_BLOCK), :], qs[step])
        parts, hides = [], []
        for i in range(low, high):
            piece = s[(i - low) * SEL_BLOCK : (i - low + 1) * SEL_BLOCK]
            start = entries[i][3]
            if i < own_blocks:
                parts.append(jnp.where(ahead <= first + step * ROWS - start, piece, -FAR))
                hides.append(None)
            else:
                parts.append(piece)
                hides.append(jnp.where(start <= first, 0.0, FAR).astype(F32))
        return parts, hides

    def near_front(step):
        parts, hides = fine_parts(step, 0, near_count)
        return parts, hides, peak(parts, hides)

    def near_back(step, parts, hides, top):
        wnear[step, : near_count * SEL_BLOCK] = weigh(parts, hides, top)
        stat[1, step, 0:1] = top

    @when(core == 1)
    def _():
        relay(1, 0)
        coarse_gather()

    half = STEPS // 2
    if near_count > 0:
        near_fronts, near_backs = spans(near_front, near_back)
        pipeline(near_fronts[:half], near_backs[:half])
    @when(core == 0)
    def _():
        relay(1, 0)
        coarse_gather()

    @when(bridge)
    def _():
        values_on().wait_recv()
        values_over().start()

    @when(core == 1)
    def _():
        relay(1, 1)

    if near_count > 0:
        pipeline(near_fronts[half:], near_backs[half:])

    chip = 2 * B * N

    def chip_rows(e):
        return pl.ds(pl.multiple_of(((y + e) % Y) * chip, chip), chip)

    k = lax.broadcasted_iota(jnp.int32, (chip, ROWS), 0)
    for e in range(Y):
        column = ((y + e) % Y) * 2 + k // (B * N)
        seen = (k % (B * N)) // N * G + column < position
        bias[pl.ds(e * chip, chip), :] = jnp.where(seen, 0.0, -FAR)

    def coarse_phase():
        kc, qc = iotas(N)
        ends = kc * CMP_BLOCK + (CMP_BLOCK - 1) - qc
        mine = pl.ds(G * B * N, N)
        each_chunk(lambda k: coarse_to_mate(0, k).wait_recv())
        cvt[:HEAD_DIM, :chip] = cc[1, chip_rows(0), :].T
        cvt[:HEAD_DIM, chip:] = cc[1, pl.ds(G * B * N, ROWS), :].T

        def coarse_front(step):
            k = jnp.concatenate([cc[0, chip_rows(0), :], cc[0, mine, :]], axis=0)
            s = scores(k, qs[step])
            parts = [
                s[:chip] + jnp.concatenate([bias[:chip, :]] * HEADS, axis=1),
                jnp.where(ends <= step * ROWS, s[chip:], -FAR),
            ]
            hides = [None] * len(parts)
            return parts, hides, jnp.maximum(peak(parts, hides), 0.0)

        def coarse_back(step, parts, hides, top):
            w = weigh(parts, hides, top)
            w = jnp.concatenate([w, jnp.zeros((ROWS - N, LANES), BF16)], axis=0)
            keep(2, step, top, *times(cvt[...], w))

        return spans(coarse_front, coarse_back)

    @when(core == 0)
    def _():
        relay(1, 1)
        pipeline(*coarse_phase())

    spread(1)

    if near_count > 0:
        near_keys = near_count * SEL_BLOCK
        for i in range(near_count):
            fv[pl.ds(i * SEL_BLOCK, SEL_BLOCK), :] = sv[entries[i][1]]
        fvt[:HEAD_DIM, :near_keys] = fv[:near_keys, :].T
        for step in range(STEPS):
            mixed, total = times(
                fvt[:, : near_count * SEL_BLOCK], wnear[step, : near_count * SEL_BLOCK]
            )
            part[1, step] = mixed
            stat[1, step, 1:2] = total

    def coarse_relay():
        def pass_on(k):
            for e in range(1, Y):
                coarse_over_y(e, k).wait_recv()
                coarse_to_mate(e, k).start()

        each_chunk(pass_on)

    @when(core == 0)
    def _():
        coarse_relay()

    @when(jnp.logical_and(g == 0, b > 0))
    def _():
        keys_on().wait_recv()
        prev_weights(pk[...].reshape(flat))

    @when(core == 1)
    def _():
        coarse_relay()
        pipeline(*coarse_phase())

    @when(jnp.logical_and(core == 0, g > 0))
    def _():
        prev_before()

    def others_in(k):
        for e in range(1, Y):
            coarse_to_mate(e, k).wait_recv()

    each_chunk(others_in)

    cvt_far[:HEAD_DIM] = jnp.concatenate([cc[1, chip_rows(e), :] for e in range(1, Y)], axis=0).T

    def coarse_far_front(step):
        k = jnp.concatenate([cc[0, chip_rows(e), :] for e in range(1, Y)], axis=0)
        off = bias[pl.ds(chip, (Y - 1) * chip), :]
        parts = [scores(k, qs[step]) + jnp.concatenate([off] * HEADS, axis=1)]
        return parts, [None], jnp.maximum(peak(parts, [None]), stat[2, step, 0:1])

    def coarse_far_back(step, parts, hides, top):
        w = weigh(parts, hides, top)
        mixed, total = join(2, step, top, *times(cvt_far[...], w))
        acc[step] = mixed * (gate(0, step) / (total + jnp.exp2(-top)))

    pipeline(*spans(coarse_far_front, coarse_far_back))

    @when(jnp.logical_and(g == 0, b > 0))
    def _():
        values_over().wait_recv()
        pvt[:HEAD_DIM] = pv[...].reshape(flat).T
        prev_product()

    @when(position == 0)
    def _():
        for step in range(STEPS):
            part[0, step] = part[0, step] * (gate(2, step) / stat[0, step, 1:2])

    for c in range(2):
        for h in halves:
            for e in range(1, Y):
                over_y(c, e, h).wait_send()
            for e in range(Y):
                to_mate(c, e, h).wait_send()

    @when(source)
    def _():
        values_on().wait_send()

    @when(crossed)
    def _():
        keys_on().wait_send()

    @when(bridge)
    def _():
        values_over().wait_send()

    for d in range(1, B):

        @when(b + d < B)
        def _(d=d):
            coarse_out(d).wait_send()
            for c in range(2):
                block_out(c, d).wait_send()

    def coarse_left(k):
        for e in range(1, Y):
            coarse_over_y(e, k).wait_send()
        for e in range(Y):
            coarse_to_mate(e, k).wait_send()

    each_chunk(coarse_left)

    for d in range(1, B):

        @when(b - d >= 0)
        def _(d=d):
            for c in range(2):
                block_out(c, d).wait_recv()

    for i in range(near_count, TOPN):
        near, rank, owner, _ = entries[i]
        fk[pl.ds(i * SEL_BLOCK, SEL_BLOCK), :] = jnp.where(near, sk[rank], ik[owner])
        fv[pl.ds(i * SEL_BLOCK, SEL_BLOCK), :] = jnp.where(near, sv[rank], iv[owner])
    fvt[:HEAD_DIM, near_count * SEL_BLOCK :] = fv[near_count * SEL_BLOCK :, :].T

    def far_front(step):
        parts, hides = fine_parts(step, near_count, TOPN)
        top = peak(parts, hides)
        if near_count > 0:
            top = jnp.maximum(top, stat[1, step, 0:1])
        return parts, hides, top

    def far_back(step, parts, hides, top):
        w = weigh(parts, hides, top)
        mixed, total = times(fvt[:, near_count * SEL_BLOCK :], w)
        if near_count > 0:
            mixed, total = join(1, step, top, mixed, total)
        mixed = (acc[step] + part[0, step] + mixed * (gate(1, step) / total)).astype(BF16)
        for h in range(HEADS):
            out[step * ROWS : (step + 1) * ROWS, h * HEAD_DIM : (h + 1) * HEAD_DIM] = mixed[
                :, h * ROWS : (h + 1) * ROWS
            ].T

    pipeline(*spans(far_front, far_back))


def per_device(
    queries, keys, values, selected, key_in, key_out, value_in, value_out, positions, gate_weight
):
    B = lax.axis_size("blk")
    G = lax.axis_size("grp")
    T = keys.shape[0]
    N = T // CMP_BLOCK
    Y = G // 2
    STEPS = T // ROWS
    own_blocks = T // SEL_BLOCK
    inner, hidden = key_in.shape
    near_keys = min(max(TOPN - (B - 1), 0), own_blocks) * SEL_BLOCK
    anywhere = pl.BlockSpec(memory_space=pl.ANY)
    dma = pltpu.SemaphoreType.DMA
    regular = pltpu.SemaphoreType.REGULAR

    def buf(*shape, dtype=BF16):
        return pltpu.VMEM(shape, dtype)

    def blocks(count):
        return buf(count, SEL_BLOCK, HEAD_DIM)

    return pl.pallas_call(
        functools.partial(kernel, B, G),
        out_shape=pltpu.VMEM(queries.shape, BF16),
        in_specs=[anywhere] * 10,
        out_specs=pl.BlockSpec(memory_space=pltpu.VMEM),
        scratch_shapes=[
            pltpu.SMEM((TOPN, B * G), jnp.int32),
            buf(*queries.shape),
            buf(*positions.shape),
            buf(gate_weight.shape[1], gate_weight.shape[0]),
            buf(2, inner, hidden),
            buf(2, hidden, HEAD_DIM),
            buf(2, T, HEAD_DIM, dtype=F32),
            blocks(G * own_blocks),
            blocks(G * own_blocks),
            blocks(own_blocks),
            blocks(own_blocks),
            blocks(B),
            blocks(B),
            blocks(B - 1),
            blocks(B - 1),
            buf(2, G * B * N + ROWS, HEAD_DIM),
            buf(TALL, 2 * B * N + ROWS),
            buf(TALL, (Y - 1) * 2 * B * N),
            buf(STEPS, 2 * HEAD_DIM, LANES),
            buf(TALL, T),
            buf(TALL, T),
            buf(TOPN * SEL_BLOCK, HEAD_DIM),
            buf(TOPN * SEL_BLOCK, HEAD_DIM),
            buf(TALL, TOPN * SEL_BLOCK),
            buf(G * B * N, ROWS, dtype=F32),
            buf(STEPS, max(near_keys, T), LANES),
            buf(STEPS, HEAD_DIM, LANES, dtype=F32),
            buf(3, STEPS, HEAD_DIM, LANES, dtype=F32),
            buf(3, STEPS, 8, LANES, dtype=F32),
            buf(3 * HEADS, T, dtype=F32),
            dma((6,)),
            dma((4,)),
            dma((2, Y, 2)),
            dma((2, Y, 2)),
            dma((2, Y, 2)),
            dma((2, Y, 2)),
            dma((3,)),
            dma((3,)),
            dma((2, B)),
            dma((2, B)),
            dma((B,)),
            dma((B,)),
            dma((2, Y, 4)),
            dma((2, Y, 4)),
            regular((B,)),
        ],
        compiler_params=pltpu.CompilerParams(
            collective_id=0, has_side_effects=True, vmem_limit_bytes=56 << 20
        ),
    )(
        selected.T,
        queries,
        keys.reshape(T // SEL_BLOCK, SEL_BLOCK, HEAD_DIM),
        values.reshape(T // SEL_BLOCK, SEL_BLOCK, HEAD_DIM),
        key_in,
        key_out,
        value_in,
        value_out,
        positions,
        gate_weight.T,
    )


def solution(mesh):
    rows = P(("blk", "grp"), None)
    return jax.shard_map(
        per_device,
        mesh=mesh,
        in_specs=(rows, rows, rows, P(), P(), P(), P(), P(), P(), P()),
        out_specs=rows,
        check_vma=False,
    )
```

```python
import functools
import math

import jax
import jax.numpy as jnp
from jax import lax
from jax.experimental import pallas as pl
from jax.experimental.pallas import tpu as pltpu
from jax.sharding import PartitionSpec as P

HEAD_DIM = 128
HEADS = 4
TALL = HEAD_DIM + 16
CMP_BLOCK = 32
SEL_BLOCK = 64
TOPN = 16
WINDOW = 512
ROWS = 128
LANES = HEADS * ROWS

FAR = 1e30
RATE = HEAD_DIM**-0.5 * math.log2(math.e)
MESH = pl.DeviceIdType.MESH
F32 = jnp.float32
BF16 = jnp.bfloat16


def across(a, b):
    return lax.dot_general(a, b, (((1,), (1,)), ((), ())), preferred_element_type=F32)


def scores(k, q):
    return jnp.dot(jnp.concatenate([k, k], axis=1), q, preferred_element_type=F32)


def rows8(s):
    return s.reshape(s.shape[0] // 8, 8, s.shape[1])


def peak(parts, hides):
    tops = []
    for s, hide in zip(parts, hides):
        top = jnp.max(rows8(s), axis=0)
        tops.append(top if hide is None else top - hide)
    return jnp.max(functools.reduce(jnp.maximum, tops), axis=0, keepdims=True)


def weigh(parts, hides, top):
    packed = []
    for s, hide in zip(parts, hides):
        w = jnp.exp2(s - (top if hide is None else top + hide))
        packed.append(w.astype(BF16))
    return jnp.concatenate(packed, axis=0)


def times(vt, w):
    both = jnp.dot(vt, w, preferred_element_type=F32)
    return both[:HEAD_DIM], both[HEAD_DIM : HEAD_DIM + 1]


def pipeline(fronts, backs):
    held = fronts[0]()
    for n, back in enumerate(backs):
        following = fronts[n + 1]() if n + 1 < len(fronts) else None
        back(*held)
        held = following


def merge_sort(keys):
    keys = list(keys)
    n = len(keys)
    p = 1
    while p < n:
        k = p
        while k >= 1:
            for j in range(k % p, n - k, 2 * k):
                for i in range(min(k, n - j - k)):
                    if (i + j) // (p * 2) == (i + j + k) // (p * 2):
                        lo, hi = keys[i + j], keys[i + j + k]
                        keys[i + j] = jnp.minimum(lo, hi)
                        keys[i + j + k] = jnp.maximum(lo, hi)
            k //= 2
        p *= 2
    return keys


def kernel(
    B,
    G,
    sel_in,
    queries_in,
    keys_in,
    values_in,
    key_in,
    key_out,
    value_in,
    value_out,
    positions_in,
    gate_weight_in,
    out,
    sel,
    queries,
    positions,
    gate_weight,
    w_in,
    w_out,
    shifted,
    sk,
    sv,
    pk,
    pv,
    ik,
    iv,
    stk,
    stv,
    cc,
    cvt,
    cvt_far,
    qs,
    wvt,
    pvt,
    fk,
    fv,
    fvt,
    bias,
    wnear,
    acc,
    part,
    stat,
    gates,
    l_sem,
    w_sem,
    a_s,
    a_r,
    m_s,
    m_r,
    p_s,
    p_r,
    b_s,
    b_r,
    c_r,
    f_s,
    f_r,
    ready,
):
    T = queries.shape[0]
    N = T // CMP_BLOCK
    Y = G // 2
    STEPS = T // ROWS
    own_blocks = T // SEL_BLOCK
    per_row = G * own_blocks
    near_count = min(max(TOPN - (B - 1), 0), own_blocks)
    b = lax.axis_index("blk")
    g = lax.axis_index("grp")
    y = g // 2
    core = g % 2
    mate = g + 1 - 2 * core
    position = b * G + g
    first = position * T

    row = (sk, sv)
    prev = (pk, pv)
    staged = (stk, stv)
    inbox = (ik, iv)

    flat = (T, HEAD_DIM)

    def slot(column):
        return pl.ds(column * own_blocks, own_blocks)

    def local(src, dst, sem):
        return pltpu.make_async_copy(src, dst, sem)

    def remote(src, dst, send, recv, dev):
        return pltpu.make_async_remote_copy(
            src_ref=src,
            dst_ref=dst,
            send_sem=send,
            recv_sem=recv,
            device_id=dev,
            device_id_type=MESH,
        )

    def at(stretch, column):
        return {"blk": stretch, "grp": column}

    def when(condition):
        return lambda body: pl.when(condition)(body)

    own_load = [
        local(keys_in, sk.at[slot(g)], l_sem.at[0]),
        local(values_in, sv.at[slot(g)], l_sem.at[1]),
    ]
    q_load = local(queries_in, queries, l_sem.at[2])
    gate_load = local(gate_weight_in, gate_weight, l_sem.at[3])
    shift_load = local(positions_in, positions, l_sem.at[4])
    sel_load = local(sel_in, sel, l_sem.at[5])
    weight_loads = [
        local(src, dst, w_sem.at[n])
        for n, (src, dst) in enumerate(
            (
                (key_in, w_in.at[0]),
                (value_in, w_in.at[1]),
                (key_out, w_out.at[0]),
                (value_out, w_out.at[1]),
            )
        )
    ]
    for load in own_load:
        load.start()
    cc[...] = jnp.zeros_like(cc)
    barrier = pltpu.get_barrier_semaphore()

    def greet(dev):
        pl.semaphore_signal(barrier, inc=1, device_id=dev, device_id_type=MESH)

    for e in range(1, G):
        greet(at(b, (g + e) % G))
    for d in range(1, B):

        @when(b + d < B)
        def _(d=d):
            greet(at(b + d, g))

    for load in [q_load, shift_load] + weight_loads[0::2] + [gate_load, sel_load]:
        load.start()


    source = jnp.logical_and(g == G - 1, b < B - 1)
    crossed = jnp.logical_and(g == 1, b < B - 1)
    bridge = jnp.logical_and(g == G - 2, b > 0)
    for load in own_load:
        load.wait()
    for load in weight_loads[1::2]:
        load.start()

    mine_rows = pl.ds(pl.multiple_of((g * B + b) * N, N), N)

    def compress(c):
        shift = positions[c].astype(F32)
        tokens = row[c][slot(g)].reshape(flat).astype(F32).reshape(N, CMP_BLOCK, HEAD_DIM)
        shifted[c] = (tokens + shift[None]).reshape(flat)
        for load in weight_loads[c::2]:
            load.wait()
        wide = jnp.concatenate(
            [shifted[c, pl.ds(t, N, stride=CMP_BLOCK), :].astype(BF16) for t in range(CMP_BLOCK)],
            axis=1,
        )
        hidden = jax.nn.silu(jnp.dot(wide, w_in[c], preferred_element_type=F32)).astype(BF16)
        mine = jnp.dot(hidden, w_out[c], preferred_element_type=F32).astype(BF16)
        cc[c, mine_rows, :] = mine
        cc[c, G * B * N : G * B * N + N, :] = mine

    shift_load.wait()

    early = jnp.logical_and(b == 0, y == 0)
    late = jnp.logical_or(b > 0, y > 0)

    @when(early)
    def _():
        compress(0)
        compress(1)

    pl.semaphore_wait(barrier, G - 1 + b)

    def piece_of(column, h):
        return pl.ds(column * own_blocks + h * (own_blocks // 2), own_blocks // 2)

    def over_y(c, e, h):
        piece = row[c].at[piece_of(g, h)]
        dev = at(b, ((y + e) % Y) * 2 + core)
        return remote(piece, piece, a_s.at[0], a_r.at[c, e - 1, h], dev)

    def to_mate(c, e, h):
        piece = row[c].at[piece_of(((y - e + Y) % Y) * 2 + core, h)]
        return remote(piece, piece, m_s.at[0], m_r.at[c if e else 0, e], at(b, mate))

    def keys_on():
        return remote(sk.at[slot(G - 1)], pk, p_s.at[0], p_r.at[0], at((b + 1) % B, 0))

    def values_on():
        return remote(sv.at[slot(G - 1)], pv, p_s.at[1], p_r.at[1], at((b + 1) % B, G - 2))

    def values_over():
        return remote(pv, pv, p_s.at[2], p_r.at[2], at(b, 0))

    def block_out(c, d):
        return remote(
            staged[c].at[d - 1], inbox[c].at[b], b_s.at[d - 1], b_r.at[d - 1], at((b + d) % B, g)
        )

    chunks = 4 if B % 4 == 0 else 1
    reach = B // chunks

    def column_rows(column, k):
        count = B // chunks * N
        return pl.ds(pl.multiple_of(column * B * N + k * count, N), count)

    def each_chunk(body):
        for k in range(chunks):

            @when(b >= k * (B // chunks))
            def _(k=k):
                body(k)

    def coarse_out(d):
        piece = cc.at[:, mine_rows, :]
        return remote(piece, piece, b_s.at[d - 1], c_r.at[d - 1], at((b + d) % B, g))

    def coarse_over_y(e, k):
        piece = cc.at[:, column_rows(g, k), :]
        dev = at(b, ((y + e) % Y) * 2 + core)
        return remote(piece, piece, f_s.at[k], f_r.at[e - 1, k], dev)

    def coarse_to_mate(e, k):
        piece = cc.at[:, column_rows(((y - e + Y) % Y) * 2 + core, k), :]
        return remote(piece, piece, f_s.at[k], f_r.at[Y - 1 + e, k], at(b, mate))

    def all_of(ref, sem):
        return local(ref, ref, sem)

    halves = range(2)
    for h in halves:
        for e in range(1, Y):
            over_y(0, e, h).start()
        to_mate(0, 0, h).start()
    for h in halves:
        to_mate(1, 0, h).start()

    for d in range(1, B):

        @when(b - d >= 0)
        def _(d=d):
            pl.semaphore_signal(ready.at[d - 1], inc=1, device_id=at(b - d, g), device_id_type=MESH)

    q_load.wait()
    for step in range(STEPS):
        for h in range(HEADS):
            piece = queries[step * ROWS : (step + 1) * ROWS, h * HEAD_DIM : (h + 1) * HEAD_DIM]
            piece = piece.T.astype(F32) * RATE
            high = piece.astype(BF16)
            qs[step, :HEAD_DIM, h * ROWS : (h + 1) * ROWS] = high
            qs[step, HEAD_DIM:, h * ROWS : (h + 1) * ROWS] = (piece - high.astype(F32)).astype(BF16)

    for turned in (wvt, pvt, cvt, cvt_far, fvt):
        turned[HEAD_DIM:, :] = jnp.ones_like(turned[HEAD_DIM:, :])
    wvt[:HEAD_DIM] = sv[slot(g)].reshape(flat).T

    def iotas(count):
        k = lax.broadcasted_iota(jnp.int32, (count, LANES), 0)
        q = lax.broadcasted_iota(jnp.int32, (count, LANES), 1) % ROWS
        return k, q

    def gate(n, step):
        cols = pl.ds(step * ROWS, ROWS)
        return jnp.concatenate(
            [gates[n * HEADS + h : n * HEADS + h + 1, cols] for h in range(HEADS)], axis=1
        )

    def keep(which, step, top, mixed, total):
        part[which, step] = mixed
        stat[which, step, 0:1] = top
        stat[which, step, 1:2] = total

    def join(which, step, best, mixed, total):
        old = jnp.exp2(stat[which, step, 0:1] - best)
        return part[which, step] * old + mixed, stat[which, step, 1:2] * old + total

    @when(late)
    def _():
        compress(0)

    @when(source)
    def _():
        pl.semaphore_wait(ready.at[0], 1)
        values_on().start()

    @when(late)
    def _():
        compress(1)

    def coarse_gather():
        for d in range(1, B):

            @when(b - d >= 0)
            def _(d=d):
                coarse_out(d).wait_recv()

        def send(k):
            for e in range(1, Y):
                coarse_over_y(e, k).start()
            coarse_to_mate(0, k).start()

        each_chunk(send)

    @when(b == 0)
    def _():
        coarse_gather()

    for h in halves:
        for e in range(1, Y):
            over_y(1, e, h).start()

    def coarse_on(low, high, which=True):
        for d in range(low, high):

            @when(jnp.logical_and(b + d < B, which))
            def _(d=d):
                if d == 1:

                    @when(g < G - 1)
                    def _():
                        pl.semaphore_wait(ready.at[d - 1], 1)
                else:
                    pl.semaphore_wait(ready.at[d - 1], 1)
                coarse_out(d).start()

    coarse_on(1, B // 2, late)

    gate_load.wait()
    gates[...] = jax.nn.sigmoid(across(gate_weight[...], queries[...]))
    sel_load.wait()

    def owner_of(j):
        return lax.div(j, per_row)

    def same(left, right):
        gap = left - right
        return 1 - jnp.minimum(jnp.maximum(gap, -gap), 1)

    picks = []
    for d in range(1, B):
        line = jnp.minimum(b + d, B - 1) * G + g
        pick = jnp.int32(0)
        for i in range(TOPN):
            j = sel[i, line]
            pick = pick + same(owner_of(j), b) * (j - b * per_row)
        picks.append(pick)

    order = []
    for i in range(TOPN):
        j = sel[i, position]
        rel = j - b * per_row - g * own_blocks
        wrapped = jnp.where(rel < 0, rel + per_row, rel)
        order.append(jnp.where(j >= b * per_row, wrapped, j + per_row))
    order = merge_sort(order)

    def entry(i):
        code = order[i]
        near = code < per_row
        turned = code + g * own_blocks
        rank = jnp.where(turned >= per_row, turned - per_row, turned)
        rank = jnp.where(near, rank, 0)
        start = jnp.where(near, (b * per_row + rank) * SEL_BLOCK, 0)
        owner = jnp.where(near, 0, owner_of(code - per_row))
        return near, rank, owner, start

    kd, qd = iotas(ROWS)
    own_keys = sk[slot(g)].reshape(flat)

    def own_front(step):
        count = (step + 1) * ROWS
        s = scores(own_keys[:count], qs[step])
        parts = [jnp.where(kd <= qd, s[count - ROWS :], -FAR)]
        if step > 0:
            parts = [s[: count - ROWS]] + parts
        hides = [None] * len(parts)
        return parts, hides, peak(parts, hides)

    def own_back(step, parts, hides, top):
        w = weigh(parts, hides, top)
        keep(0, step, top, *times(wvt[:, : (step + 1) * ROWS], w))

    def spans(front, back):
        return (
            [functools.partial(front, step) for step in range(STEPS)],
            [functools.partial(back, step) for step in range(STEPS)],
        )

    pipeline(*spans(own_front, own_back))
    coarse_on(1, B // 2, early)
    coarse_on(B // 2, B)

    def relay(c, h):
        for e in range(1, Y):
            over_y(c, e, h).wait_recv()
            to_mate(c, e, h).start()

    relay(0, 0)
    def spread(c):
        for e in range(1, Y):
            all_of(sk.at[pl.ds(0, own_blocks)], m_r.at[c, e]).wait()
        for d in range(1, B):

            @when(b + d < B)
            def _(d=d):
                staged[c][d - 1] = row[c][picks[d - 1]]

        for d in range(1, B):

            @when(b + d < B)
            def _(d=d):
                block_out(c, d).start()

    relay(0, 1)

    @when(crossed)
    def _():
        keys_on().start()

    all_of(sk.at[pl.ds(0, 2 * own_blocks)], m_r.at[0, 0]).wait()

    def prev_front(prev_keys, step):
        s = scores(prev_keys[step * ROWS :], qs[step])
        parts = [jnp.where(kd > qd, s[:ROWS], -FAR)]
        if step < STEPS - 1:
            parts.append(s[ROWS:])
        hides = [None] * len(parts)
        return parts, hides, jnp.maximum(peak(parts, hides), stat[0, step, 0:1])

    def prev_phase(prev_keys):
        def back(step, parts, hides, top):
            w = weigh(parts, hides, top)
            mixed, total = join(0, step, top, *times(pvt[:, step * ROWS :], w))
            part[0, step] = mixed * (gate(2, step) / total)

        fronts = [functools.partial(prev_front, prev_keys, step) for step in range(STEPS)]
        pipeline(fronts, [functools.partial(back, step) for step in range(STEPS)])

    def prev_weights(prev_keys):
        fronts = [functools.partial(prev_front, prev_keys, step) for step in range(STEPS)]

        def back(step, parts, hides, top):
            wnear[step, : T - step * ROWS] = weigh(parts, hides, top)
            stat[0, step, 2:3] = top

        pipeline(fronts, [functools.partial(back, step) for step in range(STEPS)])

    def prev_product():
        for step in range(STEPS):
            both = times(pvt[:, step * ROWS :], wnear[step, : T - step * ROWS])
            mixed, total = join(0, step, stat[0, step, 2:3], *both)
            part[0, step] = mixed * (gate(2, step) / total)

    def prev_before():
        before = slot((g + G - 1) % G)
        pvt[:HEAD_DIM] = sv[before].reshape(flat).T
        prev_phase(sk[before].reshape(flat))

    @when(core == 1)
    def _():
        prev_before()

    spread(0)

    entries = [entry(i) for i in range(TOPN)]
    for i in range(near_count):
        fk[pl.ds(i * SEL_BLOCK, SEL_BLOCK), :] = sk[entries[i][1]]

    ks, qf = iotas(SEL_BLOCK)
    ahead = ks - qf

    def fine_parts(step, low, high):
        s = scores(fk[pl.ds(low * SEL_BLOCK, (high - low) * SEL_BLOCK), :], qs[step])
        parts, hides = [], []
        for i in range(low, high):
            piece = s[(i - low) * SEL_BLOCK : (i - low + 1) * SEL_BLOCK]
            start = entries[i][3]
            if i < own_blocks:
                parts.append(jnp.where(ahead <= first + step * ROWS - start, piece, -FAR))
                hides.append(None)
            else:
                parts.append(piece)
                hides.append(jnp.where(start <= first, 0.0, FAR).astype(F32))
        return parts, hides

    def near_front(step):
        parts, hides = fine_parts(step, 0, near_count)
        return parts, hides, peak(parts, hides)

    def near_back(step, parts, hides, top):
        wnear[step, : near_count * SEL_BLOCK] = weigh(parts, hides, top)
        stat[1, step, 0:1] = top

    @when(core == 1)
    def _():
        relay(1, 0)

        @when(b > 0)
        def _():
            coarse_gather()


    half = STEPS // 2
    if near_count > 0:
        near_fronts, near_backs = spans(near_front, near_back)
        pipeline(near_fronts[:half], near_backs[:half])
    @when(core == 0)
    def _():
        relay(1, 0)

        @when(b > 0)
        def _():
            coarse_gather()


    @when(bridge)
    def _():
        values_on().wait_recv()
        values_over().start()

    @when(core == 1)
    def _():
        relay(1, 1)

    if near_count > 0:
        pipeline(near_fronts[half:], near_backs[half:])

    chip = 2 * B * N

    def chip_rows(e):
        return pl.ds(pl.multiple_of(((y + e) % Y) * chip, chip), chip)

    k = lax.broadcasted_iota(jnp.int32, (chip, ROWS), 0)
    for e in range(Y):
        column = ((y + e) % Y) * 2 + k // (B * N)
        seen = (k % (B * N)) // N * G + column < position
        bias[pl.ds(e * chip, chip), :] = jnp.where(seen, 0.0, -FAR)

    def coarse_phase():
        kc, qc = iotas(N)
        ends = kc * CMP_BLOCK + (CMP_BLOCK - 1) - qc
        mine = pl.ds(G * B * N, N)
        each_chunk(lambda k: coarse_to_mate(0, k).wait_recv())
        cvt[:HEAD_DIM, :chip] = cc[1, chip_rows(0), :].T
        cvt[:HEAD_DIM, chip:] = cc[1, pl.ds(G * B * N, ROWS), :].T

        def coarse_front(step):
            k = jnp.concatenate([cc[0, chip_rows(0), :], cc[0, mine, :]], axis=0)
            s = scores(k, qs[step])
            parts = [
                s[:chip] + jnp.concatenate([bias[:chip, :]] * HEADS, axis=1),
                jnp.where(ends <= step * ROWS, s[chip:], -FAR),
            ]
            hides = [None] * len(parts)
            return parts, hides, jnp.maximum(peak(parts, hides), 0.0)

        def coarse_back(step, parts, hides, top):
            w = weigh(parts, hides, top)
            w = jnp.concatenate([w, jnp.zeros((ROWS - N, LANES), BF16)], axis=0)
            keep(2, step, top, *times(cvt[...], w))

        return spans(coarse_front, coarse_back)

    @when(core == 0)
    def _():
        relay(1, 1)
        pipeline(*coarse_phase())

    spread(1)

    if near_count > 0:
        near_keys = near_count * SEL_BLOCK
        for i in range(near_count):
            fv[pl.ds(i * SEL_BLOCK, SEL_BLOCK), :] = sv[entries[i][1]]
        fvt[:HEAD_DIM, :near_keys] = fv[:near_keys, :].T
        for step in range(STEPS):
            mixed, total = times(
                fvt[:, : near_count * SEL_BLOCK], wnear[step, : near_count * SEL_BLOCK]
            )
            part[1, step] = mixed
            stat[1, step, 1:2] = total

    def coarse_relay():
        def pass_on(k):
            for e in range(1, Y):
                coarse_over_y(e, k).wait_recv()
                coarse_to_mate(e, k).start()

        each_chunk(pass_on)

    @when(core == 0)
    def _():
        coarse_relay()

    @when(jnp.logical_and(g == 0, b > 0))
    def _():
        keys_on().wait_recv()
        prev_weights(pk[...].reshape(flat))

    @when(core == 1)
    def _():
        coarse_relay()
        pipeline(*coarse_phase())

    @when(jnp.logical_and(core == 0, g > 0))
    def _():
        prev_before()

    def others_in(k):
        for e in range(1, Y):
            coarse_to_mate(e, k).wait_recv()

    each_chunk(others_in)

    cvt_far[:HEAD_DIM] = jnp.concatenate([cc[1, chip_rows(e), :] for e in range(1, Y)], axis=0).T

    def coarse_far_front(step):
        k = jnp.concatenate([cc[0, chip_rows(e), :] for e in range(1, Y)], axis=0)
        off = bias[pl.ds(chip, (Y - 1) * chip), :]
        parts = [scores(k, qs[step]) + jnp.concatenate([off] * HEADS, axis=1)]
        return parts, [None], jnp.maximum(peak(parts, [None]), stat[2, step, 0:1])

    def coarse_far_back(step, parts, hides, top):
        w = weigh(parts, hides, top)
        mixed, total = join(2, step, top, *times(cvt_far[...], w))
        acc[step] = mixed * (gate(0, step) / (total + jnp.exp2(-top)))

    pipeline(*spans(coarse_far_front, coarse_far_back))

    @when(jnp.logical_and(g == 0, b > 0))
    def _():
        values_over().wait_recv()
        pvt[:HEAD_DIM] = pv[...].reshape(flat).T
        prev_product()

    @when(position == 0)
    def _():
        for step in range(STEPS):
            part[0, step] = part[0, step] * (gate(2, step) / stat[0, step, 1:2])

    all_of(sk.at[pl.ds(0, (Y - 1) * 2 * own_blocks)], a_s.at[0]).wait()
    all_of(sk, m_s.at[0]).wait()

    @when(source)
    def _():
        values_on().wait_send()

    @when(crossed)
    def _():
        keys_on().wait_send()

    @when(bridge)
    def _():
        values_over().wait_send()

    for d in range(1, B):

        @when(b + d < B)
        def _(d=d):
            all_of(cc.at[0, pl.ds(0, 2 * (N + SEL_BLOCK)), :], b_s.at[d - 1]).wait()

    def coarse_left(k):
        all_of(cc.at[0, pl.ds(0, (2 * Y - 1) * 2 * reach * N), :], f_s.at[k]).wait()

    each_chunk(coarse_left)

    for d in range(1, B):

        @when(b - d >= 0)
        def _(d=d):
            all_of(sk.at[pl.ds(0, 2)], b_r.at[d - 1]).wait()

    for i in range(near_count, TOPN):
        near, rank, owner, _ = entries[i]
        fk[pl.ds(i * SEL_BLOCK, SEL_BLOCK), :] = jnp.where(near, sk[rank], ik[owner])
        fv[pl.ds(i * SEL_BLOCK, SEL_BLOCK), :] = jnp.where(near, sv[rank], iv[owner])
    fvt[:HEAD_DIM, near_count * SEL_BLOCK :] = fv[near_count * SEL_BLOCK :, :].T

    def far_front(step):
        parts, hides = fine_parts(step, near_count, TOPN)
        top = peak(parts, hides)
        if near_count > 0:
            top = jnp.maximum(top, stat[1, step, 0:1])
        return parts, hides, top

    def far_back(step, parts, hides, top):
        w = weigh(parts, hides, top)
        mixed, total = times(fvt[:, near_count * SEL_BLOCK :], w)
        if near_count > 0:
            mixed, total = join(1, step, top, mixed, total)
        mixed = (acc[step] + part[0, step] + mixed * (gate(1, step) / total)).astype(BF16)
        for h in range(HEADS):
            out[step * ROWS : (step + 1) * ROWS, h * HEAD_DIM : (h + 1) * HEAD_DIM] = mixed[
                :, h * ROWS : (h + 1) * ROWS
            ].T

    pipeline(*spans(far_front, far_back))


def per_device(
    queries, keys, values, selected, key_in, key_out, value_in, value_out, positions, gate_weight
):
    B = lax.axis_size("blk")
    G = lax.axis_size("grp")
    T = keys.shape[0]
    N = T // CMP_BLOCK
    Y = G // 2
    STEPS = T // ROWS
    own_blocks = T // SEL_BLOCK
    inner, hidden = key_in.shape
    near_keys = min(max(TOPN - (B - 1), 0), own_blocks) * SEL_BLOCK
    anywhere = pl.BlockSpec(memory_space=pl.ANY)
    dma = pltpu.SemaphoreType.DMA
    regular = pltpu.SemaphoreType.REGULAR

    def buf(*shape, dtype=BF16):
        return pltpu.VMEM(shape, dtype)

    def blocks(count):
        return buf(count, SEL_BLOCK, HEAD_DIM)

    return pl.pallas_call(
        functools.partial(kernel, B, G),
        out_shape=pltpu.VMEM(queries.shape, BF16),
        in_specs=[anywhere] * 10,
        out_specs=pl.BlockSpec(memory_space=pltpu.VMEM),
        scratch_shapes=[
            pltpu.SMEM((TOPN, B * G), jnp.int32),
            buf(*queries.shape),
            buf(*positions.shape),
            buf(gate_weight.shape[1], gate_weight.shape[0]),
            buf(2, inner, hidden),
            buf(2, hidden, HEAD_DIM),
            buf(2, T, HEAD_DIM, dtype=F32),
            blocks(G * own_blocks),
            blocks(G * own_blocks),
            blocks(own_blocks),
            blocks(own_blocks),
            blocks(B),
            blocks(B),
            blocks(B - 1),
            blocks(B - 1),
            buf(2, G * B * N + ROWS, HEAD_DIM),
            buf(TALL, 2 * B * N + ROWS),
            buf(TALL, (Y - 1) * 2 * B * N),
            buf(STEPS, 2 * HEAD_DIM, LANES),
            buf(TALL, T),
            buf(TALL, T),
            buf(TOPN * SEL_BLOCK, HEAD_DIM),
            buf(TOPN * SEL_BLOCK, HEAD_DIM),
            buf(TALL, TOPN * SEL_BLOCK),
            buf(G * B * N, ROWS, dtype=F32),
            buf(STEPS, max(near_keys, T), LANES),
            buf(STEPS, HEAD_DIM, LANES, dtype=F32),
            buf(3, STEPS, HEAD_DIM, LANES, dtype=F32),
            buf(3, STEPS, 8, LANES, dtype=F32),
            buf(3 * HEADS, T, dtype=F32),
            dma((6,)),
            dma((4,)),
            dma((1,)),
            dma((2, Y - 1, 2)),
            dma((1,)),
            dma((2, Y)),
            dma((3,)),
            dma((3,)),
            dma((B - 1,)),
            dma((B - 1,)),
            dma((B - 1,)),
            dma((4,)),
            dma((2 * Y - 1, 4)),
            regular((B - 1,)),
        ],
        compiler_params=pltpu.CompilerParams(
            collective_id=0, has_side_effects=True, vmem_limit_bytes=56 << 20
        ),
    )(
        selected.T,
        queries,
        keys.reshape(T // SEL_BLOCK, SEL_BLOCK, HEAD_DIM),
        values.reshape(T // SEL_BLOCK, SEL_BLOCK, HEAD_DIM),
        key_in,
        key_out,
        value_in,
        value_out,
        positions,
        gate_weight.T,
    )


def solution(mesh):
    rows = P(("blk", "grp"), None)
    return jax.shard_map(
        per_device,
        mesh=mesh,
        in_specs=(rows, rows, rows, P(), P(), P(), P(), P(), P(), P()),
        out_specs=rows,
        check_vma=False,
    )
```

```python
import functools
import math

import jax
import jax.numpy as jnp
from jax import lax
from jax.experimental import pallas as pl
from jax.experimental.pallas import tpu as pltpu
from jax.sharding import PartitionSpec as P

HEAD_DIM = 128
HEADS = 4
TALL = HEAD_DIM + 16
CMP_BLOCK = 32
SEL_BLOCK = 64
TOPN = 16
WINDOW = 512
ROWS = 128
LANES = HEADS * ROWS

FAR = 1e30
RATE = HEAD_DIM**-0.5 * math.log2(math.e)
MESH = pl.DeviceIdType.MESH
F32 = jnp.float32
BF16 = jnp.bfloat16


def across(a, b):
    return lax.dot_general(a, b, (((1,), (1,)), ((), ())), preferred_element_type=F32)


def scores(k, q):
    return jnp.dot(jnp.concatenate([k, k], axis=1), q, preferred_element_type=F32)


def rows8(s):
    return s.reshape(s.shape[0] // 8, 8, s.shape[1])


def peak(parts, hides):
    tops = []
    for s, hide in zip(parts, hides):
        top = jnp.max(rows8(s), axis=0)
        tops.append(top if hide is None else top - hide)
    return jnp.max(functools.reduce(jnp.maximum, tops), axis=0, keepdims=True)


def weigh(parts, hides, top):
    packed = []
    for s, hide in zip(parts, hides):
        w = jnp.exp2(s - (top if hide is None else top + hide))
        packed.append(w.astype(BF16))
    return jnp.concatenate(packed, axis=0)


def times(vt, w):
    both = jnp.dot(vt, w, preferred_element_type=F32)
    return both[:HEAD_DIM], both[HEAD_DIM : HEAD_DIM + 1]


def pipeline(fronts, backs):
    held = fronts[0]()
    for n, back in enumerate(backs):
        following = fronts[n + 1]() if n + 1 < len(fronts) else None
        back(*held)
        held = following


def merge_sort(keys):
    keys = list(keys)
    n = len(keys)
    p = 1
    while p < n:
        k = p
        while k >= 1:
            for j in range(k % p, n - k, 2 * k):
                for i in range(min(k, n - j - k)):
                    if (i + j) // (p * 2) == (i + j + k) // (p * 2):
                        lo, hi = keys[i + j], keys[i + j + k]
                        keys[i + j] = jnp.minimum(lo, hi)
                        keys[i + j + k] = jnp.maximum(lo, hi)
            k //= 2
        p *= 2
    return keys


def kernel(
    B,
    G,
    sel_in,
    queries_in,
    keys_in,
    values_in,
    key_in,
    key_out,
    value_in,
    value_out,
    positions_in,
    gate_weight_in,
    out,
    sel,
    queries,
    positions,
    gate_weight,
    w_in,
    w_out,
    shifted,
    sk,
    sv,
    pk,
    pv,
    ik,
    iv,
    stk,
    stv,
    cc,
    cvt,
    cvt_far,
    qs,
    wvt,
    pvt,
    fk,
    fv,
    fvt,
    bias,
    wnear,
    acc,
    part,
    stat,
    gates,
    l_sem,
    w_sem,
    a_s,
    a_r,
    m_s,
    m_r,
    p_s,
    p_r,
    b_s,
    b_r,
    c_r,
    f_s,
    f_r,
    ready,
):
    T = queries.shape[0]
    N = T // CMP_BLOCK
    Y = G // 2
    STEPS = T // ROWS
    own_blocks = T // SEL_BLOCK
    per_row = G * own_blocks
    near_count = min(max(TOPN - (B - 1), 0), own_blocks)
    b = lax.axis_index("blk")
    g = lax.axis_index("grp")
    y = g // 2
    core = g % 2
    mate = g + 1 - 2 * core
    position = b * G + g
    first = position * T

    row = (sk, sv)
    prev = (pk, pv)
    staged = (stk, stv)
    inbox = (ik, iv)

    flat = (T, HEAD_DIM)

    def slot(column):
        return pl.ds(column * own_blocks, own_blocks)

    def local(src, dst, sem):
        return pltpu.make_async_copy(src, dst, sem)

    def remote(src, dst, send, recv, dev):
        return pltpu.make_async_remote_copy(
            src_ref=src,
            dst_ref=dst,
            send_sem=send,
            recv_sem=recv,
            device_id=dev,
            device_id_type=MESH,
        )

    def at(stretch, column):
        return {"blk": stretch, "grp": column}

    def when(condition):
        return lambda body: pl.when(condition)(body)

    own_load = [
        local(keys_in, sk.at[slot(g)], l_sem.at[0]),
        local(values_in, sv.at[slot(g)], l_sem.at[1]),
    ]
    q_load = local(queries_in, queries, l_sem.at[2])
    gate_load = local(gate_weight_in, gate_weight, l_sem.at[3])
    shift_load = local(positions_in, positions, l_sem.at[4])
    sel_load = local(sel_in, sel, l_sem.at[5])
    weight_loads = [
        local(src, dst, w_sem.at[n])
        for n, (src, dst) in enumerate(
            (
                (key_in, w_in.at[0]),
                (value_in, w_in.at[1]),
                (key_out, w_out.at[0]),
                (value_out, w_out.at[1]),
            )
        )
    ]
    for load in own_load:
        load.start()
    cc[...] = jnp.zeros_like(cc)
    barrier = pltpu.get_barrier_semaphore()

    def greet(dev):
        pl.semaphore_signal(barrier, inc=1, device_id=dev, device_id_type=MESH)

    for e in range(1, G):
        greet(at(b, (g + e) % G))
    for d in range(1, B):

        @when(b + d < B)
        def _(d=d):
            greet(at(b + d, g))

    for load in [q_load, shift_load] + weight_loads[0::2] + [gate_load, sel_load]:
        load.start()


    source = jnp.logical_and(g == G - 1, b < B - 1)
    crossed = jnp.logical_and(g == 1, b < B - 1)
    bridge = jnp.logical_and(g == G - 2, b > 0)
    for load in own_load:
        load.wait()
    for load in weight_loads[1::2]:
        load.start()

    mine_rows = pl.ds(pl.multiple_of((g * B + b) * N, N), N)

    def compress(c):
        shift = positions[c].astype(F32)
        tokens = row[c][slot(g)].reshape(flat).astype(F32).reshape(N, CMP_BLOCK, HEAD_DIM)
        shifted[c] = (tokens + shift[None]).reshape(flat)
        for load in weight_loads[c::2]:
            load.wait()
        wide = jnp.concatenate(
            [shifted[c, pl.ds(t, N, stride=CMP_BLOCK), :].astype(BF16) for t in range(CMP_BLOCK)],
            axis=1,
        )
        hidden = jax.nn.silu(jnp.dot(wide, w_in[c], preferred_element_type=F32)).astype(BF16)
        mine = jnp.dot(hidden, w_out[c], preferred_element_type=F32).astype(BF16)
        cc[c, mine_rows, :] = mine
        cc[c, G * B * N : G * B * N + N, :] = mine

    shift_load.wait()

    early = jnp.logical_and(b == 0, y == 0)
    late = jnp.logical_or(b > 0, y > 0)

    @when(early)
    def _():
        compress(0)
        compress(1)

    pl.semaphore_wait(barrier, G - 1 + b)

    def piece_of(column, h):
        return pl.ds(column * own_blocks + h * (own_blocks // 2), own_blocks // 2)

    def over_y(c, e, h):
        piece = row[c].at[piece_of(g, h)]
        dev = at(b, ((y + e) % Y) * 2 + core)
        return remote(piece, piece, a_s.at[0], a_r.at[c, e - 1, h], dev)

    def to_mate(c, e, h):
        piece = row[c].at[piece_of(((y - e + Y) % Y) * 2 + core, h)]
        return remote(piece, piece, m_s.at[0], m_r.at[c if e else 0, e], at(b, mate))

    def keys_on():
        return remote(sk.at[slot(G - 1)], pk, p_s.at[0], p_r.at[0], at((b + 1) % B, 0))

    def values_on():
        return remote(sv.at[slot(G - 1)], pv, p_s.at[1], p_r.at[1], at((b + 1) % B, G - 2))

    def values_over():
        return remote(pv, pv, p_s.at[2], p_r.at[2], at(b, 0))

    def block_out(c, d):
        return remote(
            staged[c].at[d - 1], inbox[c].at[b], b_s.at[0], b_r.at[0], at((b + d) % B, g)
        )

    chunks = 4 if B % 4 == 0 else 1
    reach = B // chunks

    def column_rows(column, k):
        count = B // chunks * N
        return pl.ds(pl.multiple_of(column * B * N + k * count, N), count)

    def each_chunk(body):
        for k in range(chunks):

            @when(b >= k * (B // chunks))
            def _(k=k):
                body(k)

    def coarse_out(d):
        piece = cc.at[:, mine_rows, :]
        return remote(piece, piece, b_s.at[0], c_r.at[0], at((b + d) % B, g))

    def coarse_over_y(e, k):
        piece = cc.at[:, column_rows(g, k), :]
        dev = at(b, ((y + e) % Y) * 2 + core)
        return remote(piece, piece, f_s.at[0], f_r.at[e - 1], dev)

    def coarse_to_mate(e, k):
        piece = cc.at[:, column_rows(((y - e + Y) % Y) * 2 + core, k), :]
        return remote(piece, piece, f_s.at[0], f_r.at[Y - 1 + e], at(b, mate))

    def all_of(ref, sem):
        return local(ref, ref, sem)

    def counted(number, low, high, rows, sem):
        for n in range(low, high):

            @when(number == n)
            def _(n=n):
                all_of(w_in.at[0, pl.ds(0, n * rows), :], sem).wait()

    coarse_bytes = N
    chunk_bytes = reach * N
    block_bytes = SEL_BLOCK
    halves = range(2)
    for h in halves:
        for e in range(1, Y):
            over_y(0, e, h).start()
        to_mate(0, 0, h).start()
    for h in halves:
        to_mate(1, 0, h).start()

    for d in range(1, B):

        @when(b - d >= 0)
        def _(d=d):
            pl.semaphore_signal(ready.at[d - 1], inc=1, device_id=at(b - d, g), device_id_type=MESH)

    q_load.wait()
    for step in range(STEPS):
        for h in range(HEADS):
            piece = queries[step * ROWS : (step + 1) * ROWS, h * HEAD_DIM : (h + 1) * HEAD_DIM]
            piece = piece.T.astype(F32) * RATE
            high = piece.astype(BF16)
            qs[step, :HEAD_DIM, h * ROWS : (h + 1) * ROWS] = high
            qs[step, HEAD_DIM:, h * ROWS : (h + 1) * ROWS] = (piece - high.astype(F32)).astype(BF16)

    for turned in (wvt, pvt, cvt, cvt_far, fvt):
        turned[HEAD_DIM:, :] = jnp.ones_like(turned[HEAD_DIM:, :])
    wvt[:HEAD_DIM] = sv[slot(g)].reshape(flat).T

    def iotas(count):
        k = lax.broadcasted_iota(jnp.int32, (count, LANES), 0)
        q = lax.broadcasted_iota(jnp.int32, (count, LANES), 1) % ROWS
        return k, q

    def gate(n, step):
        cols = pl.ds(step * ROWS, ROWS)
        return jnp.concatenate(
            [gates[n * HEADS + h : n * HEADS + h + 1, cols] for h in range(HEADS)], axis=1
        )

    def keep(which, step, top, mixed, total):
        part[which, step] = mixed
        stat[which, step, 0:1] = top
        stat[which, step, 1:2] = total

    def join(which, step, best, mixed, total):
        old = jnp.exp2(stat[which, step, 0:1] - best)
        return part[which, step] * old + mixed, stat[which, step, 1:2] * old + total

    @when(late)
    def _():
        compress(0)

    @when(source)
    def _():
        pl.semaphore_wait(ready.at[0], 1)
        values_on().start()

    @when(late)
    def _():
        compress(1)

    def coarse_gather():
        counted(b, 1, B, coarse_bytes, c_r.at[0])

        def send(k):
            for e in range(1, Y):
                coarse_over_y(e, k).start()
            coarse_to_mate(0, k).start()

        each_chunk(send)

    @when(b == 0)
    def _():
        coarse_gather()

    for h in halves:
        for e in range(1, Y):
            over_y(1, e, h).start()

    def coarse_on(low, high, which=True):
        for d in range(low, high):

            @when(jnp.logical_and(b + d < B, which))
            def _(d=d):
                if d == 1:

                    @when(g < G - 1)
                    def _():
                        pl.semaphore_wait(ready.at[d - 1], 1)
                else:
                    pl.semaphore_wait(ready.at[d - 1], 1)
                coarse_out(d).start()

    coarse_on(1, B // 2, late)

    gate_load.wait()
    gates[...] = jax.nn.sigmoid(across(gate_weight[...], queries[...]))
    sel_load.wait()

    def owner_of(j):
        return lax.div(j, per_row)

    def same(left, right):
        gap = left - right
        return 1 - jnp.minimum(jnp.maximum(gap, -gap), 1)

    picks = []
    for d in range(1, B):
        line = jnp.minimum(b + d, B - 1) * G + g
        pick = jnp.int32(0)
        for i in range(TOPN):
            j = sel[i, line]
            pick = pick + same(owner_of(j), b) * (j - b * per_row)
        picks.append(pick)

    order = []
    for i in range(TOPN):
        j = sel[i, position]
        rel = j - b * per_row - g * own_blocks
        wrapped = jnp.where(rel < 0, rel + per_row, rel)
        order.append(jnp.where(j >= b * per_row, wrapped, j + per_row))
    order = merge_sort(order)

    def entry(i):
        code = order[i]
        near = code < per_row
        turned = code + g * own_blocks
        rank = jnp.where(turned >= per_row, turned - per_row, turned)
        rank = jnp.where(near, rank, 0)
        start = jnp.where(near, (b * per_row + rank) * SEL_BLOCK, 0)
        owner = jnp.where(near, 0, owner_of(code - per_row))
        return near, rank, owner, start

    kd, qd = iotas(ROWS)
    own_keys = sk[slot(g)].reshape(flat)

    def own_front(step):
        count = (step + 1) * ROWS
        s = scores(own_keys[:count], qs[step])
        parts = [jnp.where(kd <= qd, s[count - ROWS :], -FAR)]
        if step > 0:
            parts = [s[: count - ROWS]] + parts
        hides = [None] * len(parts)
        return parts, hides, peak(parts, hides)

    def own_back(step, parts, hides, top):
        w = weigh(parts, hides, top)
        keep(0, step, top, *times(wvt[:, : (step + 1) * ROWS], w))

    def spans(front, back):
        return (
            [functools.partial(front, step) for step in range(STEPS)],
            [functools.partial(back, step) for step in range(STEPS)],
        )

    pipeline(*spans(own_front, own_back))
    coarse_on(1, B // 2, early)
    coarse_on(B // 2, B)

    def relay(c, h):
        for e in range(1, Y):
            over_y(c, e, h).wait_recv()
            to_mate(c, e, h).start()

    relay(0, 0)
    def spread(c):
        for e in range(1, Y):
            all_of(sk.at[pl.ds(0, own_blocks)], m_r.at[c, e]).wait()
        for d in range(1, B):

            @when(b + d < B)
            def _(d=d):
                staged[c][d - 1] = row[c][picks[d - 1]]

        for d in range(1, B):

            @when(b + d < B)
            def _(d=d):
                block_out(c, d).start()

    relay(0, 1)

    @when(crossed)
    def _():
        keys_on().start()

    all_of(sk.at[pl.ds(0, 2 * own_blocks)], m_r.at[0, 0]).wait()

    def prev_front(prev_keys, step):
        s = scores(prev_keys[step * ROWS :], qs[step])
        parts = [jnp.where(kd > qd, s[:ROWS], -FAR)]
        if step < STEPS - 1:
            parts.append(s[ROWS:])
        hides = [None] * len(parts)
        return parts, hides, jnp.maximum(peak(parts, hides), stat[0, step, 0:1])

    def prev_phase(prev_keys):
        def back(step, parts, hides, top):
            w = weigh(parts, hides, top)
            mixed, total = join(0, step, top, *times(pvt[:, step * ROWS :], w))
            part[0, step] = mixed * (gate(2, step) / total)

        fronts = [functools.partial(prev_front, prev_keys, step) for step in range(STEPS)]
        pipeline(fronts, [functools.partial(back, step) for step in range(STEPS)])

    def prev_weights(prev_keys):
        fronts = [functools.partial(prev_front, prev_keys, step) for step in range(STEPS)]

        def back(step, parts, hides, top):
            wnear[step, : T - step * ROWS] = weigh(parts, hides, top)
            stat[0, step, 2:3] = top

        pipeline(fronts, [functools.partial(back, step) for step in range(STEPS)])

    def prev_product():
        for step in range(STEPS):
            both = times(pvt[:, step * ROWS :], wnear[step, : T - step * ROWS])
            mixed, total = join(0, step, stat[0, step, 2:3], *both)
            part[0, step] = mixed * (gate(2, step) / total)

    def prev_before():
        before = slot((g + G - 1) % G)
        pvt[:HEAD_DIM] = sv[before].reshape(flat).T
        prev_phase(sk[before].reshape(flat))

    @when(core == 1)
    def _():
        prev_before()

    spread(0)

    entries = [entry(i) for i in range(TOPN)]
    for i in range(near_count):
        fk[pl.ds(i * SEL_BLOCK, SEL_BLOCK), :] = sk[entries[i][1]]

    ks, qf = iotas(SEL_BLOCK)
    ahead = ks - qf

    def fine_parts(step, low, high):
        s = scores(fk[pl.ds(low * SEL_BLOCK, (high - low) * SEL_BLOCK), :], qs[step])
        parts, hides = [], []
        for i in range(low, high):
            piece = s[(i - low) * SEL_BLOCK : (i - low + 1) * SEL_BLOCK]
            start = entries[i][3]
            if i < own_blocks:
                parts.append(jnp.where(ahead <= first + step * ROWS - start, piece, -FAR))
                hides.append(None)
            else:
                parts.append(piece)
                hides.append(jnp.where(start <= first, 0.0, FAR).astype(F32))
        return parts, hides

    def near_front(step):
        parts, hides = fine_parts(step, 0, near_count)
        return parts, hides, peak(parts, hides)

    def near_back(step, parts, hides, top):
        wnear[step, : near_count * SEL_BLOCK] = weigh(parts, hides, top)
        stat[1, step, 0:1] = top

    @when(core == 1)
    def _():
        relay(1, 0)

        @when(b > 0)
        def _():
            coarse_gather()


    half = STEPS // 2
    if near_count > 0:
        near_fronts, near_backs = spans(near_front, near_back)
        pipeline(near_fronts[:half], near_backs[:half])
    @when(core == 0)
    def _():
        relay(1, 0)

        @when(b > 0)
        def _():
            coarse_gather()


    @when(bridge)
    def _():
        values_on().wait_recv()
        values_over().start()

    @when(core == 1)
    def _():
        relay(1, 1)

    if near_count > 0:
        pipeline(near_fronts[half:], near_backs[half:])

    chip = 2 * B * N

    def chip_rows(e):
        return pl.ds(pl.multiple_of(((y + e) % Y) * chip, chip), chip)

    k = lax.broadcasted_iota(jnp.int32, (chip, ROWS), 0)
    for e in range(Y):
        column = ((y + e) % Y) * 2 + k // (B * N)
        seen = (k % (B * N)) // N * G + column < position
        bias[pl.ds(e * chip, chip), :] = jnp.where(seen, 0.0, -FAR)

    def coarse_phase():
        kc, qc = iotas(N)
        ends = kc * CMP_BLOCK + (CMP_BLOCK - 1) - qc
        mine = pl.ds(G * B * N, N)
        counted(b // reach + 1, 1, chunks + 1, chunk_bytes, f_r.at[Y - 1])
        cvt[:HEAD_DIM, :chip] = cc[1, chip_rows(0), :].T
        cvt[:HEAD_DIM, chip:] = cc[1, pl.ds(G * B * N, ROWS), :].T

        def coarse_front(step):
            k = jnp.concatenate([cc[0, chip_rows(0), :], cc[0, mine, :]], axis=0)
            s = scores(k, qs[step])
            parts = [
                s[:chip] + jnp.concatenate([bias[:chip, :]] * HEADS, axis=1),
                jnp.where(ends <= step * ROWS, s[chip:], -FAR),
            ]
            hides = [None] * len(parts)
            return parts, hides, jnp.maximum(peak(parts, hides), 0.0)

        def coarse_back(step, parts, hides, top):
            w = weigh(parts, hides, top)
            w = jnp.concatenate([w, jnp.zeros((ROWS - N, LANES), BF16)], axis=0)
            keep(2, step, top, *times(cvt[...], w))

        return spans(coarse_front, coarse_back)

    @when(core == 0)
    def _():
        relay(1, 1)
        pipeline(*coarse_phase())

    spread(1)

    if near_count > 0:
        near_keys = near_count * SEL_BLOCK
        for i in range(near_count):
            fv[pl.ds(i * SEL_BLOCK, SEL_BLOCK), :] = sv[entries[i][1]]
        fvt[:HEAD_DIM, :near_keys] = fv[:near_keys, :].T
        for step in range(STEPS):
            mixed, total = times(
                fvt[:, : near_count * SEL_BLOCK], wnear[step, : near_count * SEL_BLOCK]
            )
            part[1, step] = mixed
            stat[1, step, 1:2] = total

    def coarse_relay():
        for e in range(1, Y):
            counted(b // reach + 1, 1, chunks + 1, chunk_bytes, f_r.at[e - 1])

        def pass_on(k):
            for e in range(1, Y):
                coarse_to_mate(e, k).start()

        each_chunk(pass_on)

    @when(core == 0)
    def _():
        coarse_relay()

    @when(jnp.logical_and(g == 0, b > 0))
    def _():
        keys_on().wait_recv()
        prev_weights(pk[...].reshape(flat))

    @when(core == 1)
    def _():
        coarse_relay()
        pipeline(*coarse_phase())

    @when(jnp.logical_and(core == 0, g > 0))
    def _():
        prev_before()

    for e in range(1, Y):
        counted(b // reach + 1, 1, chunks + 1, chunk_bytes, f_r.at[Y - 1 + e])

    cvt_far[:HEAD_DIM] = jnp.concatenate([cc[1, chip_rows(e), :] for e in range(1, Y)], axis=0).T

    def coarse_far_front(step):
        k = jnp.concatenate([cc[0, chip_rows(e), :] for e in range(1, Y)], axis=0)
        off = bias[pl.ds(chip, (Y - 1) * chip), :]
        parts = [scores(k, qs[step]) + jnp.concatenate([off] * HEADS, axis=1)]
        return parts, [None], jnp.maximum(peak(parts, [None]), stat[2, step, 0:1])

    def coarse_far_back(step, parts, hides, top):
        w = weigh(parts, hides, top)
        mixed, total = join(2, step, top, *times(cvt_far[...], w))
        acc[step] = mixed * (gate(0, step) / (total + jnp.exp2(-top)))

    pipeline(*spans(coarse_far_front, coarse_far_back))

    @when(jnp.logical_and(g == 0, b > 0))
    def _():
        values_over().wait_recv()
        pvt[:HEAD_DIM] = pv[...].reshape(flat).T
        prev_product()

    @when(position == 0)
    def _():
        for step in range(STEPS):
            part[0, step] = part[0, step] * (gate(2, step) / stat[0, step, 1:2])

    all_of(sk.at[pl.ds(0, (Y - 1) * 2 * own_blocks)], a_s.at[0]).wait()
    all_of(sk, m_s.at[0]).wait()

    @when(source)
    def _():
        values_on().wait_send()

    @when(crossed)
    def _():
        keys_on().wait_send()

    @when(bridge)
    def _():
        values_over().wait_send()

    counted(B - 1 - b, 1, B, coarse_bytes + block_bytes, b_s.at[0])
    counted(b // reach + 1, 1, chunks + 1, (2 * Y - 1) * chunk_bytes, f_s.at[0])

    counted(b, 1, B, block_bytes, b_r.at[0])

    for i in range(near_count, TOPN):
        near, rank, owner, _ = entries[i]
        fk[pl.ds(i * SEL_BLOCK, SEL_BLOCK), :] = jnp.where(near, sk[rank], ik[owner])
        fv[pl.ds(i * SEL_BLOCK, SEL_BLOCK), :] = jnp.where(near, sv[rank], iv[owner])
    fvt[:HEAD_DIM, near_count * SEL_BLOCK :] = fv[near_count * SEL_BLOCK :, :].T

    def far_front(step):
        parts, hides = fine_parts(step, near_count, TOPN)
        top = peak(parts, hides)
        if near_count > 0:
            top = jnp.maximum(top, stat[1, step, 0:1])
        return parts, hides, top

    def far_back(step, parts, hides, top):
        w = weigh(parts, hides, top)
        mixed, total = times(fvt[:, near_count * SEL_BLOCK :], w)
        if near_count > 0:
            mixed, total = join(1, step, top, mixed, total)
        mixed = (acc[step] + part[0, step] + mixed * (gate(1, step) / total)).astype(BF16)
        for h in range(HEADS):
            out[step * ROWS : (step + 1) * ROWS, h * HEAD_DIM : (h + 1) * HEAD_DIM] = mixed[
                :, h * ROWS : (h + 1) * ROWS
            ].T

    pipeline(*spans(far_front, far_back))


def per_device(
    queries, keys, values, selected, key_in, key_out, value_in, value_out, positions, gate_weight
):
    B = lax.axis_size("blk")
    G = lax.axis_size("grp")
    T = keys.shape[0]
    N = T // CMP_BLOCK
    Y = G // 2
    STEPS = T // ROWS
    own_blocks = T // SEL_BLOCK
    inner, hidden = key_in.shape
    near_keys = min(max(TOPN - (B - 1), 0), own_blocks) * SEL_BLOCK
    anywhere = pl.BlockSpec(memory_space=pl.ANY)
    dma = pltpu.SemaphoreType.DMA
    regular = pltpu.SemaphoreType.REGULAR

    def buf(*shape, dtype=BF16):
        return pltpu.VMEM(shape, dtype)

    def blocks(count):
        return buf(count, SEL_BLOCK, HEAD_DIM)

    return pl.pallas_call(
        functools.partial(kernel, B, G),
        out_shape=pltpu.VMEM(queries.shape, BF16),
        in_specs=[anywhere] * 10,
        out_specs=pl.BlockSpec(memory_space=pltpu.VMEM),
        scratch_shapes=[
            pltpu.SMEM((TOPN, B * G), jnp.int32),
            buf(*queries.shape),
            buf(*positions.shape),
            buf(gate_weight.shape[1], gate_weight.shape[0]),
            buf(2, inner, hidden),
            buf(2, hidden, HEAD_DIM),
            buf(2, T, HEAD_DIM, dtype=F32),
            blocks(G * own_blocks),
            blocks(G * own_blocks),
            blocks(own_blocks),
            blocks(own_blocks),
            blocks(B),
            blocks(B),
            blocks(B - 1),
            blocks(B - 1),
            buf(2, G * B * N + ROWS, HEAD_DIM),
            buf(TALL, 2 * B * N + ROWS),
            buf(TALL, (Y - 1) * 2 * B * N),
            buf(STEPS, 2 * HEAD_DIM, LANES),
            buf(TALL, T),
            buf(TALL, T),
            buf(TOPN * SEL_BLOCK, HEAD_DIM),
            buf(TOPN * SEL_BLOCK, HEAD_DIM),
            buf(TALL, TOPN * SEL_BLOCK),
            buf(G * B * N, ROWS, dtype=F32),
            buf(STEPS, max(near_keys, T), LANES),
            buf(STEPS, HEAD_DIM, LANES, dtype=F32),
            buf(3, STEPS, HEAD_DIM, LANES, dtype=F32),
            buf(3, STEPS, 8, LANES, dtype=F32),
            buf(3 * HEADS, T, dtype=F32),
            dma((6,)),
            dma((4,)),
            dma((1,)),
            dma((2, Y - 1, 2)),
            dma((1,)),
            dma((2, Y)),
            dma((3,)),
            dma((3,)),
            dma((1,)),
            dma((1,)),
            dma((1,)),
            dma((1,)),
            dma((2 * Y - 1,)),
            regular((B - 1,)),
        ],
        compiler_params=pltpu.CompilerParams(
            collective_id=0, has_side_effects=True, vmem_limit_bytes=56 << 20
        ),
    )(
        selected.T,
        queries,
        keys.reshape(T // SEL_BLOCK, SEL_BLOCK, HEAD_DIM),
        values.reshape(T // SEL_BLOCK, SEL_BLOCK, HEAD_DIM),
        key_in,
        key_out,
        value_in,
        value_out,
        positions,
        gate_weight.T,
    )


def solution(mesh):
    rows = P(("blk", "grp"), None)
    return jax.shard_map(
        per_device,
        mesh=mesh,
        in_specs=(rows, rows, rows, P(), P(), P(), P(), P(), P(), P()),
        out_specs=rows,
        check_vma=False,
    )
```

```python
import functools
import math

import jax
import jax.numpy as jnp
from jax import lax
from jax.experimental import pallas as pl
from jax.experimental.pallas import tpu as pltpu
from jax.sharding import PartitionSpec as P

HEAD_DIM = 128
HEADS = 4
TALL = HEAD_DIM + 16
CMP_BLOCK = 32
SEL_BLOCK = 64
TOPN = 16
WINDOW = 512
ROWS = 128
LANES = HEADS * ROWS

FAR = 1e30
RATE = HEAD_DIM**-0.5 * math.log2(math.e)
MESH = pl.DeviceIdType.MESH
F32 = jnp.float32
BF16 = jnp.bfloat16


def across(a, b):
    return lax.dot_general(a, b, (((1,), (1,)), ((), ())), preferred_element_type=F32)


def scores(k, q):
    return jnp.dot(jnp.concatenate([k, k], axis=1), q, preferred_element_type=F32)


def rows8(s):
    return s.reshape(s.shape[0] // 8, 8, s.shape[1])


def peak(parts, hides):
    tops = []
    for s, hide in zip(parts, hides):
        top = jnp.max(rows8(s), axis=0)
        tops.append(top if hide is None else top - hide)
    return jnp.max(functools.reduce(jnp.maximum, tops), axis=0, keepdims=True)


def weigh(parts, hides, top):
    packed = []
    for s, hide in zip(parts, hides):
        w = jnp.exp2(s - (top if hide is None else top + hide))
        packed.append(w.astype(BF16))
    return jnp.concatenate(packed, axis=0)


def times(vt, w):
    both = jnp.dot(vt, w, preferred_element_type=F32)
    return both[:HEAD_DIM], both[HEAD_DIM : HEAD_DIM + 1]


def pipeline(fronts, backs):
    held = fronts[0]()
    for n, back in enumerate(backs):
        following = fronts[n + 1]() if n + 1 < len(fronts) else None
        back(*held)
        held = following


def merge_sort(keys):
    keys = list(keys)
    n = len(keys)
    p = 1
    while p < n:
        k = p
        while k >= 1:
            for j in range(k % p, n - k, 2 * k):
                for i in range(min(k, n - j - k)):
                    if (i + j) // (p * 2) == (i + j + k) // (p * 2):
                        lo, hi = keys[i + j], keys[i + j + k]
                        keys[i + j] = jnp.minimum(lo, hi)
                        keys[i + j + k] = jnp.maximum(lo, hi)
            k //= 2
        p *= 2
    return keys


def kernel(
    B,
    G,
    sel_in,
    queries_in,
    keys_in,
    values_in,
    key_in,
    key_out,
    value_in,
    value_out,
    positions_in,
    gate_weight_in,
    out,
    sel,
    queries,
    positions,
    gate_weight,
    w_in,
    w_out,
    shifted,
    sk,
    sv,
    pk,
    pv,
    ik,
    iv,
    stk,
    stv,
    cc,
    cvt,
    cvt_far,
    qs,
    wvt,
    pvt,
    fk,
    fv,
    fvt,
    bias,
    wnear,
    acc,
    part,
    stat,
    gates,
    l_sem,
    w_sem,
    a_s,
    a_r,
    m_s,
    m_r,
    p_s,
    p_r,
    b_s,
    b_r,
    c_r,
    f_s,
    f_r,
    ready,
):
    T = queries.shape[0]
    N = T // CMP_BLOCK
    Y = G // 2
    STEPS = T // ROWS
    own_blocks = T // SEL_BLOCK
    per_row = G * own_blocks
    near_count = min(max(TOPN - (B - 1), 0), own_blocks)
    b = lax.axis_index("blk")
    g = lax.axis_index("grp")
    y = g // 2
    core = g % 2
    mate = g + 1 - 2 * core
    position = b * G + g
    first = position * T

    row = (sk, sv)
    prev = (pk, pv)
    staged = (stk, stv)
    inbox = (ik, iv)

    flat = (T, HEAD_DIM)

    def slot(column):
        return pl.ds(column * own_blocks, own_blocks)

    def local(src, dst, sem):
        return pltpu.make_async_copy(src, dst, sem)

    def remote(src, dst, send, recv, dev):
        return pltpu.make_async_remote_copy(
            src_ref=src,
            dst_ref=dst,
            send_sem=send,
            recv_sem=recv,
            device_id=dev,
            device_id_type=MESH,
        )

    def at(stretch, column):
        return {"blk": stretch, "grp": column}

    def when(condition):
        return lambda body: pl.when(condition)(body)

    own_load = [
        local(keys_in, sk.at[slot(g)], l_sem.at[0]),
        local(values_in, sv.at[slot(g)], l_sem.at[1]),
    ]
    q_load = local(queries_in, queries, l_sem.at[2])
    gate_load = local(gate_weight_in, gate_weight, l_sem.at[3])
    shift_load = local(positions_in, positions, l_sem.at[4])
    sel_load = local(sel_in, sel, l_sem.at[5])
    weight_loads = [
        local(src, dst, w_sem.at[n])
        for n, (src, dst) in enumerate(
            (
                (key_in, w_in.at[0]),
                (value_in, w_in.at[1]),
                (key_out, w_out.at[0]),
                (value_out, w_out.at[1]),
            )
        )
    ]
    for load in own_load:
        load.start()
    cc[...] = jnp.zeros_like(cc)
    barrier = pltpu.get_barrier_semaphore()

    def greet(dev):
        pl.semaphore_signal(barrier, inc=1, device_id=dev, device_id_type=MESH)

    for e in range(1, G):
        greet(at(b, (g + e) % G))
    for d in range(1, B):

        @when(b + d < B)
        def _(d=d):
            greet(at(b + d, g))

    for load in [q_load, shift_load] + weight_loads[0::2] + [gate_load, sel_load]:
        load.start()


    source = jnp.logical_and(g == G - 1, b < B - 1)
    crossed = jnp.logical_and(g == 1, b < B - 1)
    bridge = jnp.logical_and(g == G - 2, b > 0)
    for load in own_load:
        load.wait()
    for load in weight_loads[1::2]:
        load.start()

    mine_rows = pl.ds(pl.multiple_of((g * B + b) * N, N), N)

    def compress(c):
        shift = positions[c].astype(F32)
        tokens = row[c][slot(g)].reshape(flat).astype(F32).reshape(N, CMP_BLOCK, HEAD_DIM)
        shifted[c] = (tokens + shift[None]).reshape(flat)
        for load in weight_loads[c::2]:
            load.wait()
        wide = jnp.concatenate(
            [shifted[c, pl.ds(t, N, stride=CMP_BLOCK), :].astype(BF16) for t in range(CMP_BLOCK)],
            axis=1,
        )
        hidden = jax.nn.silu(jnp.dot(wide, w_in[c], preferred_element_type=F32)).astype(BF16)
        mine = jnp.dot(hidden, w_out[c], preferred_element_type=F32).astype(BF16)
        cc[c, mine_rows, :] = mine
        cc[c, G * B * N : G * B * N + N, :] = mine

    shift_load.wait()

    early = jnp.logical_and(b == 0, y == 0)
    late = jnp.logical_or(b > 0, y > 0)

    @when(early)
    def _():
        compress(0)
        compress(1)

    pl.semaphore_wait(barrier, G - 1 + b)

    def piece_of(column, h):
        return pl.ds(column * own_blocks + h * (own_blocks // 2), own_blocks // 2)

    def over_y(c, e, h):
        piece = row[c].at[piece_of(g, h)]
        dev = at(b, ((y + e) % Y) * 2 + core)
        return remote(piece, piece, a_s.at[0], a_r.at[c, e - 1, h], dev)

    def to_mate(c, e, h):
        piece = row[c].at[piece_of(((y - e + Y) % Y) * 2 + core, h)]
        return remote(piece, piece, m_s.at[0], m_r.at[2 * e - 1 + c if e else 0], at(b, mate))

    def keys_on():
        return remote(sk.at[slot(G - 1)], pk, p_s.at[0], p_r.at[0], at((b + 1) % B, 0))

    def values_on():
        return remote(sv.at[slot(G - 1)], pv, p_s.at[0], p_r.at[1], at((b + 1) % B, G - 2))

    def values_over():
        return remote(pv, pv, p_s.at[0], p_r.at[1], at(b, 0))

    def block_out(c, d):
        return remote(
            staged[c].at[d - 1], inbox[c].at[b], b_s.at[0], b_r.at[0], at((b + d) % B, g)
        )

    chunks = 4 if B % 4 == 0 else 1
    reach = B // chunks

    def column_rows(column, k):
        count = B // chunks * N
        return pl.ds(pl.multiple_of(column * B * N + k * count, N), count)

    def each_chunk(body):
        for k in range(chunks):

            @when(b >= k * (B // chunks))
            def _(k=k):
                body(k)

    def coarse_out(d):
        piece = cc.at[:, mine_rows, :]
        return remote(piece, piece, b_s.at[0], c_r.at[0], at((b + d) % B, g))

    def coarse_over_y(e, k):
        piece = cc.at[:, column_rows(g, k), :]
        dev = at(b, ((y + e) % Y) * 2 + core)
        return remote(piece, piece, f_s.at[0], f_r.at[e - 1], dev)

    def coarse_to_mate(e, k):
        piece = cc.at[:, column_rows(((y - e + Y) % Y) * 2 + core, k), :]
        return remote(piece, piece, f_s.at[0], f_r.at[Y - 1 + e], at(b, mate))

    def all_of(ref, sem):
        return local(ref, ref, sem)

    def counted(number, low, high, rows, sem):
        for n in range(low, high):

            @when(number == n)
            def _(n=n):
                all_of(w_in.at[0, pl.ds(0, n * rows), :], sem).wait()

    coarse_bytes = N
    chunk_bytes = reach * N
    block_bytes = SEL_BLOCK
    halves = range(2)
    for h in halves:
        for e in range(1, Y):
            over_y(0, e, h).start()
        to_mate(0, 0, h).start()
    for h in halves:
        to_mate(1, 0, h).start()

    for d in range(1, B):

        @when(b - d >= 0)
        def _(d=d):
            pl.semaphore_signal(ready.at[d - 1], inc=1, device_id=at(b - d, g), device_id_type=MESH)

    q_load.wait()
    for step in range(STEPS):
        for h in range(HEADS):
            piece = queries[step * ROWS : (step + 1) * ROWS, h * HEAD_DIM : (h + 1) * HEAD_DIM]
            piece = piece.T.astype(F32) * RATE
            high = piece.astype(BF16)
            qs[step, :HEAD_DIM, h * ROWS : (h + 1) * ROWS] = high
            qs[step, HEAD_DIM:, h * ROWS : (h + 1) * ROWS] = (piece - high.astype(F32)).astype(BF16)

    for turned in (wvt, pvt, cvt, cvt_far, fvt):
        turned[HEAD_DIM:, :] = jnp.ones_like(turned[HEAD_DIM:, :])
    wvt[:HEAD_DIM] = sv[slot(g)].reshape(flat).T

    def iotas(count):
        k = lax.broadcasted_iota(jnp.int32, (count, LANES), 0)
        q = lax.broadcasted_iota(jnp.int32, (count, LANES), 1) % ROWS
        return k, q

    def gate(n, step):
        cols = pl.ds(step * ROWS, ROWS)
        return jnp.concatenate(
            [gates[n * HEADS + h : n * HEADS + h + 1, cols] for h in range(HEADS)], axis=1
        )

    def keep(which, step, top, mixed, total):
        part[which, step] = mixed
        stat[which, step, 0:1] = top
        stat[which, step, 1:2] = total

    def join(which, step, best, mixed, total):
        old = jnp.exp2(stat[which, step, 0:1] - best)
        return part[which, step] * old + mixed, stat[which, step, 1:2] * old + total

    @when(late)
    def _():
        compress(0)

    @when(source)
    def _():
        pl.semaphore_wait(ready.at[0], 1)
        values_on().start()

    @when(late)
    def _():
        compress(1)

    def coarse_gather():
        counted(b, 1, B, coarse_bytes, c_r.at[0])

        def send(k):
            for e in range(1, Y):
                coarse_over_y(e, k).start()
            coarse_to_mate(0, k).start()

        each_chunk(send)

    @when(b == 0)
    def _():
        coarse_gather()

    for h in halves:
        for e in range(1, Y):
            over_y(1, e, h).start()

    def coarse_on(low, high, which=True):
        for d in range(low, high):

            @when(jnp.logical_and(b + d < B, which))
            def _(d=d):
                if d == 1:

                    @when(g < G - 1)
                    def _():
                        pl.semaphore_wait(ready.at[d - 1], 1)
                else:
                    pl.semaphore_wait(ready.at[d - 1], 1)
                coarse_out(d).start()

    coarse_on(1, B // 2, late)

    gate_load.wait()
    gates[...] = jax.nn.sigmoid(across(gate_weight[...], queries[...]))
    sel_load.wait()

    def owner_of(j):
        return lax.div(j, per_row)

    def same(left, right):
        gap = left - right
        return 1 - jnp.minimum(jnp.maximum(gap, -gap), 1)

    picks = []
    for d in range(1, B):
        line = jnp.minimum(b + d, B - 1) * G + g
        pick = jnp.int32(0)
        for i in range(TOPN):
            j = sel[i, line]
            pick = pick + same(owner_of(j), b) * (j - b * per_row)
        picks.append(pick)

    order = []
    for i in range(TOPN):
        j = sel[i, position]
        rel = j - b * per_row - g * own_blocks
        wrapped = jnp.where(rel < 0, rel + per_row, rel)
        order.append(jnp.where(j >= b * per_row, wrapped, j + per_row))
    order = merge_sort(order)

    def entry(i):
        code = order[i]
        near = code < per_row
        turned = code + g * own_blocks
        rank = jnp.where(turned >= per_row, turned - per_row, turned)
        rank = jnp.where(near, rank, 0)
        start = jnp.where(near, (b * per_row + rank) * SEL_BLOCK, 0)
        owner = jnp.where(near, 0, owner_of(code - per_row))
        return near, rank, owner, start

    kd, qd = iotas(ROWS)
    own_keys = sk[slot(g)].reshape(flat)

    def own_front(step):
        count = (step + 1) * ROWS
        s = scores(own_keys[:count], qs[step])
        parts = [jnp.where(kd <= qd, s[count - ROWS :], -FAR)]
        if step > 0:
            parts = [s[: count - ROWS]] + parts
        hides = [None] * len(parts)
        return parts, hides, peak(parts, hides)

    def own_back(step, parts, hides, top):
        w = weigh(parts, hides, top)
        keep(0, step, top, *times(wvt[:, : (step + 1) * ROWS], w))

    def spans(front, back):
        return (
            [functools.partial(front, step) for step in range(STEPS)],
            [functools.partial(back, step) for step in range(STEPS)],
        )

    pipeline(*spans(own_front, own_back))
    coarse_on(1, B // 2, early)
    coarse_on(B // 2, B)

    def relay(c, h):
        for e in range(1, Y):
            over_y(c, e, h).wait_recv()
            to_mate(c, e, h).start()

    relay(0, 0)
    def spread(c):
        for e in range(1, Y):
            all_of(sk.at[pl.ds(0, own_blocks)], m_r.at[2 * e - 1 + c]).wait()
        for d in range(1, B):

            @when(b + d < B)
            def _(d=d):
                staged[c][d - 1] = row[c][picks[d - 1]]

        for d in range(1, B):

            @when(b + d < B)
            def _(d=d):
                block_out(c, d).start()

    relay(0, 1)

    @when(crossed)
    def _():
        keys_on().start()

    all_of(sk.at[pl.ds(0, 2 * own_blocks)], m_r.at[0]).wait()

    def prev_front(prev_keys, step):
        s = scores(prev_keys[step * ROWS :], qs[step])
        parts = [jnp.where(kd > qd, s[:ROWS], -FAR)]
        if step < STEPS - 1:
            parts.append(s[ROWS:])
        hides = [None] * len(parts)
        return parts, hides, jnp.maximum(peak(parts, hides), stat[0, step, 0:1])

    def prev_phase(prev_keys):
        def back(step, parts, hides, top):
            w = weigh(parts, hides, top)
            mixed, total = join(0, step, top, *times(pvt[:, step * ROWS :], w))
            part[0, step] = mixed * (gate(2, step) / total)

        fronts = [functools.partial(prev_front, prev_keys, step) for step in range(STEPS)]
        pipeline(fronts, [functools.partial(back, step) for step in range(STEPS)])

    def prev_weights(prev_keys):
        fronts = [functools.partial(prev_front, prev_keys, step) for step in range(STEPS)]

        def back(step, parts, hides, top):
            wnear[step, : T - step * ROWS] = weigh(parts, hides, top)
            stat[0, step, 2:3] = top

        pipeline(fronts, [functools.partial(back, step) for step in range(STEPS)])

    def prev_product():
        for step in range(STEPS):
            both = times(pvt[:, step * ROWS :], wnear[step, : T - step * ROWS])
            mixed, total = join(0, step, stat[0, step, 2:3], *both)
            part[0, step] = mixed * (gate(2, step) / total)

    def prev_before():
        before = slot((g + G - 1) % G)
        pvt[:HEAD_DIM] = sv[before].reshape(flat).T
        prev_phase(sk[before].reshape(flat))

    @when(core == 1)
    def _():
        prev_before()

    spread(0)

    entries = [entry(i) for i in range(TOPN)]
    for i in range(near_count):
        fk[pl.ds(i * SEL_BLOCK, SEL_BLOCK), :] = sk[entries[i][1]]

    ks, qf = iotas(SEL_BLOCK)
    ahead = ks - qf

    def fine_parts(step, low, high):
        s = scores(fk[pl.ds(low * SEL_BLOCK, (high - low) * SEL_BLOCK), :], qs[step])
        parts, hides = [], []
        for i in range(low, high):
            piece = s[(i - low) * SEL_BLOCK : (i - low + 1) * SEL_BLOCK]
            start = entries[i][3]
            if i < own_blocks:
                parts.append(jnp.where(ahead <= first + step * ROWS - start, piece, -FAR))
                hides.append(None)
            else:
                parts.append(piece)
                hides.append(jnp.where(start <= first, 0.0, FAR).astype(F32))
        return parts, hides

    def near_front(step):
        parts, hides = fine_parts(step, 0, near_count)
        return parts, hides, peak(parts, hides)

    def near_back(step, parts, hides, top):
        wnear[step, : near_count * SEL_BLOCK] = weigh(parts, hides, top)
        stat[1, step, 0:1] = top

    @when(core == 1)
    def _():
        relay(1, 0)

        @when(b > 0)
        def _():
            coarse_gather()


    half = STEPS // 2
    if near_count > 0:
        near_fronts, near_backs = spans(near_front, near_back)
        pipeline(near_fronts[:half], near_backs[:half])
    @when(core == 0)
    def _():
        relay(1, 0)

        @when(b > 0)
        def _():
            coarse_gather()


    @when(bridge)
    def _():
        values_on().wait_recv()
        values_over().start()

    @when(core == 1)
    def _():
        relay(1, 1)

    if near_count > 0:
        pipeline(near_fronts[half:], near_backs[half:])

    chip = 2 * B * N

    def chip_rows(e):
        return pl.ds(pl.multiple_of(((y + e) % Y) * chip, chip), chip)

    k = lax.broadcasted_iota(jnp.int32, (chip, ROWS), 0)
    for e in range(Y):
        column = ((y + e) % Y) * 2 + k // (B * N)
        seen = (k % (B * N)) // N * G + column < position
        bias[pl.ds(e * chip, chip), :] = jnp.where(seen, 0.0, -FAR)

    def coarse_phase():
        kc, qc = iotas(N)
        ends = kc * CMP_BLOCK + (CMP_BLOCK - 1) - qc
        mine = pl.ds(G * B * N, N)
        counted(b // reach + 1, 1, chunks + 1, chunk_bytes, f_r.at[Y - 1])
        cvt[:HEAD_DIM, :chip] = cc[1, chip_rows(0), :].T
        cvt[:HEAD_DIM, chip:] = cc[1, pl.ds(G * B * N, ROWS), :].T

        def coarse_front(step):
            k = jnp.concatenate([cc[0, chip_rows(0), :], cc[0, mine, :]], axis=0)
            s = scores(k, qs[step])
            parts = [
                s[:chip] + jnp.concatenate([bias[:chip, :]] * HEADS, axis=1),
                jnp.where(ends <= step * ROWS, s[chip:], -FAR),
            ]
            hides = [None] * len(parts)
            return parts, hides, jnp.maximum(peak(parts, hides), 0.0)

        def coarse_back(step, parts, hides, top):
            w = weigh(parts, hides, top)
            w = jnp.concatenate([w, jnp.zeros((ROWS - N, LANES), BF16)], axis=0)
            keep(2, step, top, *times(cvt[...], w))

        return spans(coarse_front, coarse_back)

    @when(core == 0)
    def _():
        relay(1, 1)
        pipeline(*coarse_phase())

    spread(1)

    if near_count > 0:
        near_keys = near_count * SEL_BLOCK
        for i in range(near_count):
            fv[pl.ds(i * SEL_BLOCK, SEL_BLOCK), :] = sv[entries[i][1]]
        fvt[:HEAD_DIM, :near_keys] = fv[:near_keys, :].T
        for step in range(STEPS):
            mixed, total = times(
                fvt[:, : near_count * SEL_BLOCK], wnear[step, : near_count * SEL_BLOCK]
            )
            part[1, step] = mixed
            stat[1, step, 1:2] = total

    def coarse_relay():
        for e in range(1, Y):
            counted(b // reach + 1, 1, chunks + 1, chunk_bytes, f_r.at[e - 1])

        def pass_on(k):
            for e in range(1, Y):
                coarse_to_mate(e, k).start()

        each_chunk(pass_on)

    @when(core == 0)
    def _():
        coarse_relay()

    @when(jnp.logical_and(g == 0, b > 0))
    def _():
        keys_on().wait_recv()
        prev_weights(pk[...].reshape(flat))

    @when(core == 1)
    def _():
        coarse_relay()
        pipeline(*coarse_phase())

    @when(jnp.logical_and(core == 0, g > 0))
    def _():
        prev_before()

    for e in range(1, Y):
        counted(b // reach + 1, 1, chunks + 1, chunk_bytes, f_r.at[Y - 1 + e])

    cvt_far[:HEAD_DIM] = jnp.concatenate([cc[1, chip_rows(e), :] for e in range(1, Y)], axis=0).T

    def coarse_far_front(step):
        k = jnp.concatenate([cc[0, chip_rows(e), :] for e in range(1, Y)], axis=0)
        off = bias[pl.ds(chip, (Y - 1) * chip), :]
        parts = [scores(k, qs[step]) + jnp.concatenate([off] * HEADS, axis=1)]
        return parts, [None], jnp.maximum(peak(parts, [None]), stat[2, step, 0:1])

    def coarse_far_back(step, parts, hides, top):
        w = weigh(parts, hides, top)
        mixed, total = join(2, step, top, *times(cvt_far[...], w))
        acc[step] = mixed * (gate(0, step) / (total + jnp.exp2(-top)))

    pipeline(*spans(coarse_far_front, coarse_far_back))

    @when(jnp.logical_and(g == 0, b > 0))
    def _():
        values_over().wait_recv()
        pvt[:HEAD_DIM] = pv[...].reshape(flat).T
        prev_product()

    @when(position == 0)
    def _():
        for step in range(STEPS):
            part[0, step] = part[0, step] * (gate(2, step) / stat[0, step, 1:2])

    all_of(sk.at[pl.ds(0, (Y - 1) * 2 * own_blocks)], a_s.at[0]).wait()
    all_of(sk, m_s.at[0]).wait()

    @when(source)
    def _():
        values_on().wait_send()

    @when(crossed)
    def _():
        keys_on().wait_send()

    @when(bridge)
    def _():
        values_over().wait_send()

    counted(B - 1 - b, 1, B, coarse_bytes + block_bytes, b_s.at[0])
    counted(b // reach + 1, 1, chunks + 1, (2 * Y - 1) * chunk_bytes, f_s.at[0])

    counted(b, 1, B, block_bytes, b_r.at[0])

    for i in range(near_count, TOPN):
        near, rank, owner, _ = entries[i]
        fk[pl.ds(i * SEL_BLOCK, SEL_BLOCK), :] = jnp.where(near, sk[rank], ik[owner])
        fv[pl.ds(i * SEL_BLOCK, SEL_BLOCK), :] = jnp.where(near, sv[rank], iv[owner])
    fvt[:HEAD_DIM, near_count * SEL_BLOCK :] = fv[near_count * SEL_BLOCK :, :].T

    def far_front(step):
        parts, hides = fine_parts(step, near_count, TOPN)
        top = peak(parts, hides)
        if near_count > 0:
            top = jnp.maximum(top, stat[1, step, 0:1])
        return parts, hides, top

    def far_back(step, parts, hides, top):
        w = weigh(parts, hides, top)
        mixed, total = times(fvt[:, near_count * SEL_BLOCK :], w)
        if near_count > 0:
            mixed, total = join(1, step, top, mixed, total)
        mixed = (acc[step] + part[0, step] + mixed * (gate(1, step) / total)).astype(BF16)
        for h in range(HEADS):
            out[step * ROWS : (step + 1) * ROWS, h * HEAD_DIM : (h + 1) * HEAD_DIM] = mixed[
                :, h * ROWS : (h + 1) * ROWS
            ].T

    pipeline(*spans(far_front, far_back))


def per_device(
    queries, keys, values, selected, key_in, key_out, value_in, value_out, positions, gate_weight
):
    B = lax.axis_size("blk")
    G = lax.axis_size("grp")
    T = keys.shape[0]
    N = T // CMP_BLOCK
    Y = G // 2
    STEPS = T // ROWS
    own_blocks = T // SEL_BLOCK
    inner, hidden = key_in.shape
    near_keys = min(max(TOPN - (B - 1), 0), own_blocks) * SEL_BLOCK
    anywhere = pl.BlockSpec(memory_space=pl.ANY)
    dma = pltpu.SemaphoreType.DMA
    regular = pltpu.SemaphoreType.REGULAR

    def buf(*shape, dtype=BF16):
        return pltpu.VMEM(shape, dtype)

    def blocks(count):
        return buf(count, SEL_BLOCK, HEAD_DIM)

    return pl.pallas_call(
        functools.partial(kernel, B, G),
        out_shape=pltpu.VMEM(queries.shape, BF16),
        in_specs=[anywhere] * 10,
        out_specs=pl.BlockSpec(memory_space=pltpu.VMEM),
        scratch_shapes=[
            pltpu.SMEM((TOPN, B * G), jnp.int32),
            buf(*queries.shape),
            buf(*positions.shape),
            buf(gate_weight.shape[1], gate_weight.shape[0]),
            buf(2, inner, hidden),
            buf(2, hidden, HEAD_DIM),
            buf(2, T, HEAD_DIM, dtype=F32),
            blocks(G * own_blocks),
            blocks(G * own_blocks),
            blocks(own_blocks),
            blocks(own_blocks),
            blocks(B),
            blocks(B),
            blocks(B - 1),
            blocks(B - 1),
            buf(2, G * B * N + ROWS, HEAD_DIM),
            buf(TALL, 2 * B * N + ROWS),
            buf(TALL, (Y - 1) * 2 * B * N),
            buf(STEPS, 2 * HEAD_DIM, LANES),
            buf(TALL, T),
            buf(TALL, T),
            buf(TOPN * SEL_BLOCK, HEAD_DIM),
            buf(TOPN * SEL_BLOCK, HEAD_DIM),
            buf(TALL, TOPN * SEL_BLOCK),
            buf(G * B * N, ROWS, dtype=F32),
            buf(STEPS, max(near_keys, T), LANES),
            buf(STEPS, HEAD_DIM, LANES, dtype=F32),
            buf(3, STEPS, HEAD_DIM, LANES, dtype=F32),
            buf(3, STEPS, 8, LANES, dtype=F32),
            buf(3 * HEADS, T, dtype=F32),
            dma((6,)),
            dma((4,)),
            dma((1,)),
            dma((2, Y - 1, 2)),
            dma((1,)),
            dma((2 * Y - 1,)),
            dma((1,)),
            dma((2,)),
            dma((1,)),
            dma((1,)),
            dma((1,)),
            dma((1,)),
            dma((2 * Y - 1,)),
            regular((B - 1,)),
        ],
        compiler_params=pltpu.CompilerParams(
            collective_id=0, has_side_effects=True, vmem_limit_bytes=56 << 20
        ),
    )(
        selected.T,
        queries,
        keys.reshape(T // SEL_BLOCK, SEL_BLOCK, HEAD_DIM),
        values.reshape(T // SEL_BLOCK, SEL_BLOCK, HEAD_DIM),
        key_in,
        key_out,
        value_in,
        value_out,
        positions,
        gate_weight.T,
    )


def solution(mesh):
    rows = P(("blk", "grp"), None)
    return jax.shard_map(
        per_device,
        mesh=mesh,
        in_specs=(rows, rows, rows, P(), P(), P(), P(), P(), P(), P()),
        out_specs=rows,
        check_vma=False,
    )
```
